512 devices in a mesh: rows: 64 (over y, x, core), grp: 8 (over z).
Axes of the slice: x: 4, y: 8, z: 8, core: 2. Of those that a mesh axis runs over, the one named last changes fastest.
Arguments:
- panel_block: float32 [98304, 512], P(('rows', 'grp')), may hold values from -1000 to 1000, as said below
- trailing: float32 [98304, 768], P(('rows', 'grp')), may hold values from -1000 to 1000
Outputs:
- r_factor: float32 [512, 512], replicated
- updated_trailing: float32 [98304, 768], P(('rows', 'grp'))
The draws below stay inside these ranges and needn't reach their ends.
Inputs may be any that keep to these rules, and one draw needn't show every extreme that they name: panel_block has full column rank and is well conditioned.
All inputs are finite; a program needn't handle non-finite values.
Results may differ from the reference program's by a relative error of at most 0.000092.
Values sent between devices are 32-bit elements; how exact they have to be, the bound alone decides.
No kernel may reach another device: no remote copies, remote signals or barrier semaphores. Data moves between devices by JAX's collectives and lax.ppermute only.
A program may use at most 64 MiB of HBM per device.

```python
import math
import jax
import jax.numpy as jnp
from jax import lax

P_SIZE = 512
C = 768
ROWS = 98304


def shared_draw(key):
    base = jax.random.fold_in(key, 7)
    keys = jax.random.split(base, 5)
    position = jnp.arange(ROWS, dtype=jnp.float32) / ROWS
    row_scale = (1.0 + 2.0 * position) * jax.random.uniform(keys[0], (ROWS,), jnp.float32, 0.5, 1.5)
    column_scale = jax.random.uniform(keys[1], (P_SIZE,), jnp.float32, 0.5, 1.5)
    panel_values = jax.random.normal(keys[2], (ROWS, P_SIZE), jnp.float32) * row_scale[:, None] * column_scale[None, :]
    mixing = jax.random.normal(keys[3], (P_SIZE, C), jnp.float32) / math.sqrt(P_SIZE)
    noise = jax.random.normal(keys[4], (ROWS, C), jnp.float32) * row_scale[:, None]
    trailing_values = jnp.dot(panel_values / column_scale[None, :], mixing) + noise
    return (jnp.clip(panel_values, -1000.0, 1000.0), jnp.clip(trailing_values, -1000.0, 1000.0))


def draw_panel_block(key, part):
    return shared_draw(key)[0]


def draw_trailing(key, part):
    return shared_draw(key)[1]


def setup_inputs(seed: int = 0) -> dict:
    splits = jax.random.split(jax.random.key(seed), 3)
    return {
        "panel_block": draw_panel_block(jax.random.fold_in(splits[2], 71), 0),
        "trailing": draw_trailing(jax.random.fold_in(splits[2], 71), 0),
    }


def reference(panel_block, trailing):
    highest = lax.Precision.HIGHEST
    row_count = panel_block.shape[0]
    gram = jnp.dot(panel_block.T.astype(jnp.float32), panel_block.astype(jnp.float32), precision=highest, preferred_element_type=jnp.float32) / row_count
    lower_factor = jnp.linalg.cholesky(gram)
    orthogonal = jax.scipy.linalg.solve_triangular(lower_factor, panel_block.T, lower=True).T
    projected = jnp.dot(orthogonal.T.astype(jnp.float32), trailing.astype(jnp.float32), precision=highest, preferred_element_type=jnp.float32) / row_count
    updated_trailing = trailing - jnp.dot(orthogonal.astype(jnp.float32), projected.astype(jnp.float32), precision=highest, preferred_element_type=jnp.float32)
    return (lower_factor.T, updated_trailing)
```

```python
import jax
import jax.numpy as jnp
from jax import lax
from jax.experimental import pallas as pl
from jax.experimental.pallas import tpu as pltpu
from jax.sharding import Mesh, PartitionSpec as P

HI = lax.Precision.HIGHEST
B = 128
NP = 4
NC = 6
G_BLOCKS = [(i, j) for i in range(NP) for j in range(i, NP)]
C_BLOCKS = [(i, j) for i in range(NP) for j in range(NC)]
G_HALF = 6
C_HALF = 12


def split_half(blocks, half):
    n = (len(blocks) + 1) // 2
    return [(b, 0 if k < n else 1, k if k < n else k - n) for k, b in enumerate(blocks)]


def gram_kernel(core_ref, a_ref, t_ref, gk_ref, gs_ref, ck_ref, cs_ref):
    core = core_ref[0]
    at = a_ref[...].T

    def put(value, owner, slot, keep_ref, send_ref):
        rows = pl.ds(slot * B, B)

        @pl.when(core == owner)
        def _():
            keep_ref[rows, :] = value

        @pl.when(core != owner)
        def _():
            send_ref[rows, :] = value

    for (i, j), owner, slot in split_half(G_BLOCKS, G_HALF):
        value = jnp.dot(at[i * B : (i + 1) * B], a_ref[:, j * B : (j + 1) * B], precision=HI, preferred_element_type=jnp.float32)
        put(value, owner, slot, gk_ref, gs_ref)
    for ref in (gk_ref, gs_ref):
        ref[(G_HALF - 1) * B :, :] = jnp.zeros((B, B), jnp.float32)
    for (i, j), owner, slot in split_half(C_BLOCKS, C_HALF):
        value = jnp.dot(at[i * B : (i + 1) * B], t_ref[:, j * B : (j + 1) * B], precision=HI, preferred_element_type=jnp.float32)
        put(value, owner, slot, ck_ref, cs_ref)


def gram(core, a, t):
    g = jax.ShapeDtypeStruct((G_HALF * B, B), jnp.float32)
    c = jax.ShapeDtypeStruct((C_HALF * B, B), jnp.float32)
    vmem = pl.BlockSpec(memory_space=pltpu.VMEM)
    return pl.pallas_call(
        gram_kernel,
        out_shape=(g, g, c, c),
        in_specs=[pl.BlockSpec(memory_space=pltpu.SMEM), vmem, vmem],
        out_specs=[vmem] * 4,
        cost_estimate=pl.CostEstimate(flops=2 * 192 * 512 * 1280, bytes_accessed=4 << 20, transcendentals=0),
    )(core, a, t)


def diag_factor(load, store_u, store_e):
    s = [load(g) for g in range(16)]
    lane = lax.broadcasted_iota(jnp.int32, (8, B), 1)
    sub = lax.broadcasted_iota(jnp.int32, (8, B), 0)
    e = [jnp.where(lane == sub + 8 * g, 1.0, 0.0).astype(jnp.float32) for g in range(16)]
    for g0 in range(16):
        us, es = [], []
        for t in range(8):
            j = 8 * g0 + t
            cols = [jnp.broadcast_to(s[g][:, j : j + 1], (8, B)) for g in range(g0, 16)]
            inv = lax.rsqrt(jnp.broadcast_to(cols[0][t : t + 1, :], (8, B)))
            u = jnp.broadcast_to(s[g0][t : t + 1, :], (8, B)) * inv
            v = jnp.broadcast_to(e[g0][t : t + 1, :], (8, B)) * inv
            us.append(u)
            es.append(v)
            for g in range(g0, 16):
                l = cols[g - g0] * inv
                if g == g0:
                    l = jnp.where(sub > t, l, 0.0)
                s[g] = s[g] - l * u
                e[g] = e[g] - l * v
        u, v = us[0], es[0]
        for t in range(1, 8):
            u = jnp.where(sub == t, us[t], u)
            v = jnp.where(sub == t, es[t], v)
        store_u(g0, jnp.where(lane >= sub + 8 * g0, u, 0.0))
        store_e(g0, v)


def dot(x, y):
    return jnp.dot(x, y, precision=HI, preferred_element_type=jnp.float32)


def dot_t(x, y):
    return lax.dot_general(x, y, (((0,), (0,)), ((), ())), precision=HI, preferred_element_type=jnp.float32)


def panel_step(k, x, rkk, lkk):
    r0 = k * B
    r1 = r0 + B

    def store_u(g, v):
        rkk[8 * g : 8 * g + 8, :] = v

    def store_e(g, v):
        lkk[8 * g : 8 * g + 8, :] = v

    diag_factor(lambda g: x[r0 + 8 * g : r0 + 8 * g + 8, r0:r1], store_u, store_e)
    linv = lkk[...]
    if k > 0:
        x[r0:r1, :r0] = dot(linv, x[r0:r1, :r0])
    if k < NP - 1:
        x[r0:r1, r1:] = dot(linv, x[r0:r1, r1:])
    x[r0:r1, r0:r1] = linv
    for i in range(k + 1, NP):
        c0 = i * B
        left = x[r0:r1, c0 : c0 + B]
        x[c0 : c0 + B, c0:] = x[c0 : c0 + B, c0:] - dot_t(left, x[r0:r1, c0:])
        low = dot_t(left, x[r0:r1, :r1])
        if k > 0:
            x[c0 : c0 + B, :r0] = x[c0 : c0 + B, :r0] - low[:, :r0]
        x[c0 : c0 + B, r0:r1] = -low[:, r0:]


def first_kernel(row_count, core_ref, gm_ref, go_ref, x_ref, r_ref, lkk):
    core = core_ref[0]
    scale = 1.0 / row_count
    x_ref[...] = jnp.zeros_like(x_ref)
    for (i, j), owner, slot in split_half(G_BLOCKS, G_HALF):
        rows = slice(slot * B, (slot + 1) * B)
        value = jnp.where(core == owner, gm_ref[rows, :], go_ref[rows, :])
        x_ref[i * B : (i + 1) * B, j * B : (j + 1) * B] = value * scale
    panel_step(0, x_ref, r_ref, lkk)


def mid_kernel(k, xi_ref, x_ref, r_ref, lkk):
    x_ref[...] = xi_ref[...]
    panel_step(k, x_ref, r_ref, lkk)


def last_kernel(xi_ref, ra_ref, rb_ref, rc_ref, x_ref, r_ref, rkk, lkk):
    x_ref[...] = xi_ref[...]
    panel_step(NP - 1, x_ref, rkk, lkk)
    r_ref[...] = jnp.zeros_like(r_ref)
    for i, ref in enumerate((ra_ref, rb_ref, rc_ref, rkk)):
        r_ref[i * B : (i + 1) * B, i * B : (i + 1) * B] = ref[...]
        if i < NP - 1:
            r_ref[i * B : (i + 1) * B, (i + 1) * B :] = x_ref[i * B : (i + 1) * B, (i + 1) * B :]


VM = pl.BlockSpec(memory_space=pltpu.VMEM)
SM = pl.BlockSpec(memory_space=pltpu.SMEM)


def factor(row_count, core, gm, go):
    full = jax.ShapeDtypeStruct((NP * B, NP * B), jnp.float32)
    block = jax.ShapeDtypeStruct((B, B), jnp.float32)
    scratch = pltpu.VMEM((B, B), jnp.float32)
    cost = pl.CostEstimate(flops=20_000_000_000, bytes_accessed=2 << 20, transcendentals=0)
    x, ra = pl.pallas_call(
        lambda *refs: first_kernel(row_count, *refs),
        out_shape=(full, block), in_specs=[SM, VM, VM], out_specs=[VM, VM],
        scratch_shapes=[scratch], cost_estimate=cost, name="factor0",
    )(core, gm, go)
    diag = [ra]
    for k in (1, 2):
        x, rk = pl.pallas_call(
            lambda *refs, k=k: mid_kernel(k, *refs),
            out_shape=(full, block), in_specs=[VM], out_specs=[VM, VM],
            scratch_shapes=[scratch], cost_estimate=cost, name=f"factor{k}",
        )(x)
        diag.append(rk)
    return pl.pallas_call(
        last_kernel,
        out_shape=(full, full), in_specs=[VM] * 4, out_specs=[VM, VM],
        scratch_shapes=[scratch, scratch], cost_estimate=cost, name="factor3",
    )(x, *diag)


def update_kernel(row_count, core_ref, x_ref, cm_ref, co_ref, a_ref, t_ref, out_ref, q, p):
    core = core_ref[0]
    scale = 1.0 / row_count
    for i in range(NP):
        li = x_ref[i * B : (i + 1) * B, : (i + 1) * B]
        q[:, i * B : (i + 1) * B] = lax.dot_general(
            a_ref[:, : (i + 1) * B], li, (((1,), (1,)), ((), ())), precision=HI, preferred_element_type=jnp.float32
        )
    c = {}
    for b, owner, slot in split_half(C_BLOCKS, C_HALF):
        rows = slice(slot * B, (slot + 1) * B)
        c[b] = jnp.where(core == owner, cm_ref[rows, :], co_ref[rows, :]) * scale
    for j in range(NC):
        col = jnp.concatenate([c[(i, j)] for i in range(NP)], axis=0)
        for i in range(NP):
            p[i * B : (i + 1) * B, j * B : (j + 1) * B] = dot(x_ref[i * B : (i + 1) * B, : (i + 1) * B], col[: (i + 1) * B])
    for j in range(NC):
        cols = slice(j * B, (j + 1) * B)
        out_ref[:, cols] = t_ref[:, cols] - dot(q[...], p[:, cols])


def update(row_count, core, x, cm, co, a, t):
    return pl.pallas_call(
        lambda *refs: update_kernel(row_count, *refs),
        out_shape=jax.ShapeDtypeStruct(t.shape, jnp.float32),
        in_specs=[SM] + [VM] * 5, out_specs=VM,
        scratch_shapes=[pltpu.VMEM(a.shape, jnp.float32), pltpu.VMEM((NP * B, NC * B), jnp.float32)],
        cost_estimate=pl.CostEstimate(flops=4_000_000_000, bytes_accessed=4 << 20, transcendentals=0), name="update",
    )(core, x, cm, co, a, t)


def reduce_all(keep, send):
    half = keep + lax.ppermute(send, "c", [(0, 1), (1, 0)])
    n = half.shape[0] // 32
    parts = lax.all_to_all(half.reshape(32, n, B), ("y", "x"), 0, 0)
    mine = jnp.sum(parts, axis=0)
    parts = lax.all_to_all(jnp.broadcast_to(mine[None], (8, n, B)), "z", 0, 0)
    mine = jnp.sum(parts, axis=0)
    half = lax.all_to_all(jnp.broadcast_to(mine[None], (32, n, B)), ("y", "x"), 0, 0)
    mine = half.reshape(32 * n, B)
    return mine, lax.ppermute(mine, "c", [(0, 1), (1, 0)])


def local(row_count, panel_block, trailing):
    core = lax.axis_index("c").astype(jnp.int32).reshape(1)
    gk, gs, ck, cs = gram(core, panel_block, trailing)
    gm, go = reduce_all(gk, gs)
    cm, co = reduce_all(ck, cs)
    x, r = factor(row_count, core, gm, go)
    return r, update(row_count, core, x, cm, co, panel_block, trailing)


def solution(mesh):
    fine = Mesh(mesh.devices.reshape(8, 4, 2, 8), ("y", "x", "c", "z"))
    axes = ("y", "x", "c", "z")

    def run(panel_block, trailing):
        rows = panel_block.shape[0]
        f = jax.shard_map(
            lambda a, t: local(rows, a, t),
            mesh=fine,
            in_specs=(P(axes, None), P(axes, None)),
            out_specs=(P(), P(axes, None)),
            check_vma=False,
        )
        return f(panel_block, trailing)

    return run
```

```python
import jax
import jax.numpy as jnp
from jax import lax
from jax.experimental import pallas as pl
from jax.experimental.pallas import tpu as pltpu
from jax.sharding import Mesh, PartitionSpec as P

HI = lax.Precision.HIGHEST
B = 128
NP = 4
NC = 6
G_BLOCKS = [(i, j) for i in range(NP) for j in range(i, NP)]
C_BLOCKS = [(i, j) for i in range(NP) for j in range(NC)]
G_HALF = 6
C_HALF = 12
VM = pl.BlockSpec(memory_space=pltpu.VMEM)
SM = pl.BlockSpec(memory_space=pltpu.SMEM)


def split_half(blocks):
    n = (len(blocks) + 1) // 2
    return [(b, 0 if k < n else 1, k if k < n else k - n) for k, b in enumerate(blocks)]


PARTS = 32
G_ROWS = G_HALF * B // PARTS
C_ROWS = C_HALF * B // PARTS


def gram_kernel(core_ref, a_ref, t_ref, keep_ref, send_ref):
    g_place = {b: (owner, slot) for b, owner, slot in split_half(G_BLOCKS)}
    c_place = {b: (owner, slot) for b, owner, slot in split_half(C_BLOCKS)}

    def put(ref, value, slot, start, rows):
        for p in range(0, B, 8):
            part, at = divmod(slot * B + p, rows)
            ref[part, start + at : start + at + 8, :] = value[p : p + 8]

    def fill(me):
        refs = (keep_ref, send_ref) if me == 0 else (send_ref, keep_ref)
        for i in range(NP):
            left = a_ref[:, i * B : (i + 1) * B]
            g = dot_t(left, a_ref[:, i * B :])
            for j in range(i, NP):
                owner, slot = g_place[(i, j)]
                put(refs[owner], g[:, (j - i) * B : (j - i + 1) * B], slot, 0, G_ROWS)
            c = dot_t(left, t_ref[...])
            for j in range(NC):
                owner, slot = c_place[(i, j)]
                put(refs[owner], c[:, j * B : (j + 1) * B], slot, G_ROWS, C_ROWS)
        for ref in refs:
            put(ref, jnp.zeros((B, B), jnp.float32), G_HALF - 1, 0, G_ROWS)

    for me in range(2):
        pl.when(core_ref[0] == me)(lambda me=me: fill(me))


def gram(core, a, t):
    out = jax.ShapeDtypeStruct((PARTS, G_ROWS + C_ROWS, B), jnp.float32)
    return pl.pallas_call(
        gram_kernel,
        out_shape=(out, out),
        in_specs=[SM, VM, VM],
        out_specs=[VM] * 2,
        cost_estimate=pl.CostEstimate(flops=2 * 192 * 512 * 1280, bytes_accessed=4 << 20, transcendentals=0),
        name="gram",
    )(core, a, t)


def stack_pieces(u, order):
    high = u.astype(jnp.bfloat16).astype(jnp.float32)
    rest = u - high
    mid = rest.astype(jnp.bfloat16).astype(jnp.float32)
    part = (high, mid, rest - mid)
    return jnp.concatenate([part[k] for k in order], axis=0).astype(jnp.bfloat16)


LEFT = (0, 0, 1, 0, 2, 1)
RIGHT = (0, 1, 0, 2, 0, 1)


def row_of(v, t):
    return jnp.broadcast_to(v[t : t + 1, :], v.shape)


def eliminate_rows(w_rows, v_rows, base):
    sub = lax.broadcasted_iota(jnp.int32, (8, B), 0)
    d = {}
    for k in range(8):
        col = jnp.take_along_axis(w_rows, jnp.full((8, B), base + k, jnp.int32), axis=1, mode="promise_in_bounds")
        for i in range(k + 1):
            d[i, k] = row_of(col, i)
    w = [row_of(w_rows, t) for t in range(8)]
    v = [row_of(v_rows, t) for t in range(8)]
    for t in range(8):
        inv = lax.rsqrt(d[t, t])
        u = {k: d[t, k] * inv for k in range(t + 1, 8)}
        for i in range(t + 1, 8):
            for k in range(i, 8):
                d[i, k] = d[i, k] - u[i] * u[k]
        w[t] = w[t] * inv
        v[t] = v[t] * inv
        for i in range(t + 1, 8):
            w[i] = w[i] - u[i] * w[t]
            v[i] = v[i] - u[i] * v[t]
    wo, vo = w[0], v[0]
    for t in range(1, 8):
        wo = jnp.where(sub == t, w[t], wo)
        vo = jnp.where(sub == t, v[t], vo)
    return wo, vo


def diag_factor(s, e, rkk):
    lane = lax.broadcasted_iota(jnp.int32, (8, B), 1)
    sub = lax.broadcasted_iota(jnp.int32, (8, B), 0)
    e[...] = jnp.where(
        lax.broadcasted_iota(jnp.int32, (B, B), 0) == lax.broadcasted_iota(jnp.int32, (B, B), 1), 1.0, 0.0
    ).astype(jnp.float32)

    def body(g, _):
        base = pl.multiple_of(g * 8, 8)
        rows = pl.ds(base, 8)
        u, v = eliminate_rows(s[rows, :], e[rows, :], base)
        rkk[rows, :] = jnp.where(lane >= sub + base, u, 0.0)
        left = stack_pieces(jnp.where(lane >= base + 8, u, 0.0), LEFT)
        right = jnp.concatenate([stack_pieces(u, RIGHT), stack_pieces(v, RIGHT)], axis=1)
        change = lax.dot_general(left, right, (((0,), (0,)), ((), ())), preferred_element_type=jnp.float32)
        s[...] = s[...] - change[:, :B]
        e[...] = e[...] - change[:, B:]
        e[rows, :] = v
        return 0

    lax.fori_loop(0, B // 8, body, 0)


def dot(x, y):
    return jnp.dot(x, y, precision=HI, preferred_element_type=jnp.float32)


def dot_t(x, y):
    return lax.dot_general(x, y, (((0,), (0,)), ((), ())), precision=HI, preferred_element_type=jnp.float32)


def panel_step(k, x, rkk, s, lkk):
    r0 = k * B
    r1 = r0 + B
    s[...] = x[r0:r1, r0:r1]
    diag_factor(s, lkk, rkk)
    linv = lkk[...]
    if k > 0:
        x[r0:r1, :r0] = dot(linv, x[r0:r1, :r0])
    if k < NP - 1:
        x[r0:r1, r1:] = dot(linv, x[r0:r1, r1:])
    x[r0:r1, r0:r1] = linv
    for i in range(k + 1, NP):
        c0 = i * B
        left = x[r0:r1, c0 : c0 + B]
        x[c0 : c0 + B, c0:] = x[c0 : c0 + B, c0:] - dot_t(left, x[r0:r1, c0:])
        low = dot_t(left, x[r0:r1, :r1])
        if k > 0:
            x[c0 : c0 + B, :r0] = x[c0 : c0 + B, :r0] - low[:, :r0]
        x[c0 : c0 + B, r0:r1] = -low[:, r0:]


def first_kernel(row_count, core_ref, gm_ref, go_ref, x_ref, r_ref, s, lkk):
    core = core_ref[0]
    scale = 1.0 / row_count
    x_ref[...] = jnp.zeros_like(x_ref)
    for (i, j), owner, slot in split_half(G_BLOCKS):
        rows = slice(slot * B, (slot + 1) * B)
        value = jnp.where(core == owner, gm_ref[rows, :], go_ref[rows, :])
        x_ref[i * B : (i + 1) * B, j * B : (j + 1) * B] = value * scale
    panel_step(0, x_ref, r_ref, s, lkk)


def mid_kernel(k, xi_ref, x_ref, r_ref, s, lkk):
    x_ref[...] = xi_ref[...]
    panel_step(k, x_ref, r_ref, s, lkk)


def last_kernel(xi_ref, ra_ref, rb_ref, rc_ref, x_ref, r_ref, rkk, s, lkk):
    x_ref[...] = xi_ref[...]
    panel_step(NP - 1, x_ref, rkk, s, lkk)
    r_ref[...] = jnp.zeros_like(r_ref)
    for i, ref in enumerate((ra_ref, rb_ref, rc_ref, rkk)):
        r_ref[i * B : (i + 1) * B, i * B : (i + 1) * B] = ref[...]
        if i < NP - 1:
            r_ref[i * B : (i + 1) * B, (i + 1) * B :] = x_ref[i * B : (i + 1) * B, (i + 1) * B :]


def factor(row_count, core, gm, go):
    full = jax.ShapeDtypeStruct((NP * B, NP * B), jnp.float32)
    block = jax.ShapeDtypeStruct((B, B), jnp.float32)
    scratch = pltpu.VMEM((B, B), jnp.float32)
    cost = pl.CostEstimate(flops=4_000_000_000, bytes_accessed=2 << 20, transcendentals=0)
    x, ra = pl.pallas_call(
        lambda *refs: first_kernel(row_count, *refs),
        out_shape=(full, block), in_specs=[SM, VM, VM], out_specs=[VM, VM],
        scratch_shapes=[scratch] * 2, cost_estimate=cost, name="factor0",
    )(core, gm, go)
    diag = [ra]
    for k in (1, 2):
        x, rk = pl.pallas_call(
            lambda *refs, k=k: mid_kernel(k, *refs),
            out_shape=(full, block), in_specs=[VM], out_specs=[VM, VM],
            scratch_shapes=[scratch] * 2, cost_estimate=cost,
        )(x)
        diag.append(rk)
    return pl.pallas_call(
        last_kernel,
        out_shape=(full, full), in_specs=[VM] * 4, out_specs=[VM, VM],
        scratch_shapes=[scratch] * 3, cost_estimate=cost, name="factor3",
    )(x, *diag)


def update_kernel(row_count, core_ref, x_ref, cm_ref, co_ref, a_ref, t_ref, out_ref, q, p):
    core = core_ref[0]
    scale = 1.0 / row_count
    for i in range(NP):
        li = x_ref[i * B : (i + 1) * B, : (i + 1) * B]
        q[:, i * B : (i + 1) * B] = lax.dot_general(
            a_ref[:, : (i + 1) * B], li, (((1,), (1,)), ((), ())), precision=HI, preferred_element_type=jnp.float32
        )
    c = {}
    for b, owner, slot in split_half(C_BLOCKS):
        rows = slice(slot * B, (slot + 1) * B)
        c[b] = jnp.where(core == owner, cm_ref[rows, :], co_ref[rows, :]) * scale
    for j in range(NC):
        col = jnp.concatenate([c[(i, j)] for i in range(NP)], axis=0)
        for i in range(NP):
            p[i * B : (i + 1) * B, j * B : (j + 1) * B] = dot(x_ref[i * B : (i + 1) * B, : (i + 1) * B], col[: (i + 1) * B])
    for j in range(NC):
        cols = slice(j * B, (j + 1) * B)
        out_ref[:, cols] = t_ref[:, cols] - dot(q[...], p[:, cols])


def update(row_count, core, x, cm, co, a, t):
    return pl.pallas_call(
        lambda *refs: update_kernel(row_count, *refs),
        out_shape=jax.ShapeDtypeStruct(t.shape, jnp.float32),
        in_specs=[SM] + [VM] * 5, out_specs=VM,
        scratch_shapes=[pltpu.VMEM(a.shape, jnp.float32), pltpu.VMEM((NP * B, NC * B), jnp.float32)],
        cost_estimate=pl.CostEstimate(flops=4_000_000_000, bytes_accessed=4 << 20, transcendentals=0), name="update",
    )(core, x, cm, co, a, t)


def reduce_over_devices(keep, send):
    half = keep + lax.ppermute(send, "c", [(0, 1), (1, 0)])
    mine = jnp.sum(lax.all_to_all(half, ("y", "x"), 0, 0), axis=0)
    parts = lax.all_to_all(jnp.broadcast_to(mine[None], (8,) + mine.shape), "z", 0, 0)
    return jnp.sum(parts, axis=0)


def spread(mine):
    half = lax.all_to_all(jnp.broadcast_to(mine[None], (PARTS,) + mine.shape), ("y", "x"), 0, 0)
    half = half.reshape(-1, B)
    return half, lax.ppermute(half, "c", [(0, 1), (1, 0)])


def local(row_count, panel_block, trailing):
    core = lax.axis_index("c").astype(jnp.int32).reshape(1)
    mine = reduce_over_devices(*gram(core, panel_block, trailing))
    gm, go = spread(mine[:G_ROWS])
    cm, co = spread(mine[G_ROWS:])
    x, r = factor(row_count, core, gm, go)
    return r, update(row_count, core, x, cm, co, panel_block, trailing)


def solution(mesh):
    fine = Mesh(mesh.devices.reshape(8, 4, 2, 8), ("y", "x", "c", "z"))
    axes = ("y", "x", "c", "z")

    def run(panel_block, trailing):
        rows = panel_block.shape[0]
        f = jax.shard_map(
            lambda a, t: local(rows, a, t),
            mesh=fine,
            in_specs=(P(axes, None), P(axes, None)),
            out_specs=(P(), P(axes, None)),
            check_vma=False,
        )
        return f(panel_block, trailing)

    return run
```

```python
import jax
import jax.numpy as jnp
from jax import lax
from jax.experimental import pallas as pl
from jax.experimental.pallas import tpu as pltpu
from jax.sharding import Mesh, PartitionSpec as P

HI = lax.Precision.HIGHEST
B = 128
NP = 4
NC = 6
G_BLOCKS = [(i, j) for i in range(NP) for j in range(i, NP)]
C_BLOCKS = [(i, j) for i in range(NP) for j in range(NC)]
G_HALF = 6
C_HALF = 12
VM = pl.BlockSpec(memory_space=pltpu.VMEM)
SM = pl.BlockSpec(memory_space=pltpu.SMEM)


def split_half(blocks):
    n = (len(blocks) + 1) // 2
    return [(b, 0 if k < n else 1, k if k < n else k - n) for k, b in enumerate(blocks)]


PARTS = 32
G_ROWS = G_HALF * B // PARTS
C_ROWS = C_HALF * B // PARTS


def gram_kernel(core_ref, a_ref, t_ref, keep_ref, send_ref):
    g_place = {b: (owner, slot) for b, owner, slot in split_half(G_BLOCKS)}
    c_place = {b: (owner, slot) for b, owner, slot in split_half(C_BLOCKS)}

    def put(ref, value, slot, start, rows):
        for p in range(0, B, 8):
            part, at = divmod(slot * B + p, rows)
            ref[part, start + at : start + at + 8, :] = value[p : p + 8]

    def fill(me):
        refs = (keep_ref, send_ref) if me == 0 else (send_ref, keep_ref)
        for i in range(NP):
            left = a_ref[:, i * B : (i + 1) * B]
            g = dot_t(left, a_ref[:, i * B :])
            for j in range(i, NP):
                owner, slot = g_place[(i, j)]
                put(refs[owner], g[:, (j - i) * B : (j - i + 1) * B], slot, 0, G_ROWS)
            c = dot_t(left, t_ref[...])
            for j in range(NC):
                owner, slot = c_place[(i, j)]
                put(refs[owner], c[:, j * B : (j + 1) * B], slot, G_ROWS, C_ROWS)
        for ref in refs:
            put(ref, jnp.zeros((B, B), jnp.float32), G_HALF - 1, 0, G_ROWS)

    for me in range(2):
        pl.when(core_ref[0] == me)(lambda me=me: fill(me))


def gram(core, a, t):
    out = jax.ShapeDtypeStruct((PARTS, G_ROWS + C_ROWS, B), jnp.float32)
    return pl.pallas_call(
        gram_kernel,
        out_shape=(out, out),
        in_specs=[SM, VM, VM],
        out_specs=[VM] * 2,
        cost_estimate=pl.CostEstimate(flops=2 * 192 * 512 * 1280, bytes_accessed=4 << 20, transcendentals=0),
        name="gram",
    )(core, a, t)


def stack_pieces(u, order):
    high = u.astype(jnp.bfloat16).astype(jnp.float32)
    rest = u - high
    mid = rest.astype(jnp.bfloat16).astype(jnp.float32)
    part = (high, mid, rest - mid)
    return jnp.concatenate([part[k] for k in order], axis=0).astype(jnp.bfloat16)


LEFT = (0, 0, 1, 0, 2, 1)
RIGHT = (0, 1, 0, 2, 0, 1)


def row_of(v, t):
    return jnp.broadcast_to(v[t : t + 1, :], v.shape)


def eliminate_rows(w_rows, v_rows, base):
    sub = lax.broadcasted_iota(jnp.int32, (8, B), 0)
    d = {}
    for k in range(8):
        col = jnp.take_along_axis(w_rows, jnp.full((8, B), base + k, jnp.int32), axis=1, mode="promise_in_bounds")
        for i in range(k + 1):
            d[i, k] = row_of(col, i)
    w = [row_of(w_rows, t) for t in range(8)]
    v = [row_of(v_rows, t) for t in range(8)]
    for t in range(8):
        inv = lax.rsqrt(d[t, t])
        u = {k: d[t, k] * inv for k in range(t + 1, 8)}
        for i in range(t + 1, 8):
            for k in range(i, 8):
                d[i, k] = d[i, k] - u[i] * u[k]
        w[t] = w[t] * inv
        v[t] = v[t] * inv
        for i in range(t + 1, 8):
            w[i] = w[i] - u[i] * w[t]
            v[i] = v[i] - u[i] * v[t]
    wo, vo = w[0], v[0]
    for t in range(1, 8):
        wo = jnp.where(sub == t, w[t], wo)
        vo = jnp.where(sub == t, v[t], vo)
    return wo, vo


def diag_factor(s, e, rkk):
    lane = lax.broadcasted_iota(jnp.int32, (8, B), 1)
    sub = lax.broadcasted_iota(jnp.int32, (8, B), 0)
    e[...] = jnp.where(
        lax.broadcasted_iota(jnp.int32, (B, B), 0) == lax.broadcasted_iota(jnp.int32, (B, B), 1), 1.0, 0.0
    ).astype(jnp.float32)

    def body(g, _):
        base = pl.multiple_of(g * 8, 8)
        rows = pl.ds(base, 8)
        u, v = eliminate_rows(s[rows, :], e[rows, :], base)
        rkk[rows, :] = jnp.where(lane >= sub + base, u, 0.0)
        left = stack_pieces(jnp.where(lane >= base + 8, u, 0.0), LEFT)
        right = jnp.concatenate([stack_pieces(u, RIGHT), stack_pieces(v, RIGHT)], axis=1)
        change = lax.dot_general(left, right, (((0,), (0,)), ((), ())), preferred_element_type=jnp.float32)
        s[...] = s[...] - change[:, :B]
        e[...] = e[...] - change[:, B:]
        e[rows, :] = v
        return 0

    lax.fori_loop(0, B // 8, body, 0)


def dot(x, y):
    return jnp.dot(x, y, precision=HI, preferred_element_type=jnp.float32)


def dot_t(x, y):
    return lax.dot_general(x, y, (((0,), (0,)), ((), ())), precision=HI, preferred_element_type=jnp.float32)


def panel_step(k, x, rkk, s, lkk):
    r0 = k * B
    r1 = r0 + B
    s[...] = x[r0:r1, r0:r1]
    diag_factor(s, lkk, rkk)
    linv = lkk[...]
    if k > 0:
        x[r0:r1, :r0] = dot(linv, x[r0:r1, :r0])
    if k < NP - 1:
        x[r0:r1, r1:] = dot(linv, x[r0:r1, r1:])
    x[r0:r1, r0:r1] = linv
    for i in range(k + 1, NP):
        c0 = i * B
        left = x[r0:r1, c0 : c0 + B]
        x[c0 : c0 + B, c0:] = x[c0 : c0 + B, c0:] - dot_t(left, x[r0:r1, c0:])
        low = dot_t(left, x[r0:r1, :r1])
        if k > 0:
            x[c0 : c0 + B, :r0] = x[c0 : c0 + B, :r0] - low[:, :r0]
        x[c0 : c0 + B, r0:r1] = -low[:, r0:]


LAST = NP - 1


def first_kernel(row_count, core_ref, gm_ref, go_ref, x_ref, d_ref, s, lkk):
    scale = 1.0 / row_count
    for me in range(2):

        @pl.when(core_ref[0] == me)
        def _(me=me):
            refs = (gm_ref, go_ref) if me == 0 else (go_ref, gm_ref)
            for (i, j), owner, slot in split_half(G_BLOCKS):
                x_ref[i * B : (i + 1) * B, j * B : (j + 1) * B] = refs[owner][slot * B : (slot + 1) * B, :] * scale

    for i in range(NP):
        for j in range(i):
            x_ref[i * B : (i + 1) * B, j * B : (j + 1) * B] = jnp.zeros((B, B), jnp.float32)
    for k in range(LAST):
        panel_step(k, x_ref, d_ref.at[pl.ds(k * B, B), :], s, lkk)


def last_kernel(xi_ref, d_ref, li_ref, r_ref, rkk, s, lkk):
    r0 = LAST * B
    for i in range(LAST):
        rows = slice(i * B, (i + 1) * B)
        r_ref[rows, :] = xi_ref[rows, :]
        r_ref[rows, rows] = d_ref[rows, :]
        if i > 0:
            r_ref[rows, : i * B] = jnp.zeros((B, i * B), jnp.float32)
    li_ref[...] = xi_ref[...]
    panel_step(LAST, li_ref, rkk, s, lkk)
    r_ref[r0:, :r0] = jnp.zeros((B, r0), jnp.float32)
    r_ref[r0:, r0:] = rkk[...]
    for i in (0, 2):
        li_ref[i * B : (i + 1) * B, (i + 1) * B : (i + 2) * B] = jnp.zeros((B, B), jnp.float32)


def factor(row_count, core, gm, go):
    full = jax.ShapeDtypeStruct((NP * B, NP * B), jnp.float32)
    scratch = pltpu.VMEM((B, B), jnp.float32)
    cost = pl.CostEstimate(flops=4_000_000_000, bytes_accessed=2 << 20, transcendentals=0)
    x, d = pl.pallas_call(
        lambda *refs: first_kernel(row_count, *refs),
        out_shape=(full, jax.ShapeDtypeStruct((LAST * B, B), jnp.float32)), in_specs=[SM, VM, VM], out_specs=[VM, VM],
        scratch_shapes=[scratch] * 2, cost_estimate=cost, name="factor0",
    )(core, gm, go)
    return pl.pallas_call(
        last_kernel,
        out_shape=(full, full), in_specs=[VM] * 2, out_specs=[VM, VM],
        scratch_shapes=[scratch] * 3, cost_estimate=cost, name="factor3",
    )(x, d)


def update_kernel(row_count, core_ref, x_ref, cm_ref, co_ref, a_ref, t_ref, out_ref, c, q, p):
    scale = 1.0 / row_count
    h = NP * B // 2
    for me in range(2):

        @pl.when(core_ref[0] == me)
        def _(me=me):
            refs = (cm_ref, co_ref) if me == 0 else (co_ref, cm_ref)
            for (i, j), owner, slot in split_half(C_BLOCKS):
                c[i * B : (i + 1) * B, j * B : (j + 1) * B] = refs[owner][slot * B : (slot + 1) * B, :] * scale

    for r0 in (0, h):
        r1 = r0 + h
        q[:, r0:r1] = lax.dot_general(
            a_ref[:, :r1], x_ref[r0:r1, :r1], (((1,), (1,)), ((), ())), precision=HI, preferred_element_type=jnp.float32
        )
        p[r0:r1, :] = dot(x_ref[r0:r1, :r1], c[:r1, :])
    out_ref[...] = t_ref[...] - dot(q[...], p[...])


def update(row_count, core, x, cm, co, a, t):
    wide = pltpu.VMEM((NP * B, NC * B), jnp.float32)
    return pl.pallas_call(
        lambda *refs: update_kernel(row_count, *refs),
        out_shape=jax.ShapeDtypeStruct(t.shape, jnp.float32),
        in_specs=[SM] + [VM] * 5, out_specs=VM,
        scratch_shapes=[wide, pltpu.VMEM(a.shape, jnp.float32), wide],
        cost_estimate=pl.CostEstimate(flops=4_000_000_000, bytes_accessed=4 << 20, transcendentals=0), name="update",
    )(core, x, cm, co, a, t)


ALL = ("y", "x", "c", "z")


def device(y, x, c, z):
    return ((y * 4 + x) * 2 + c) * 8 + z


PLANES = [[device(y, x, 0, z) for y in range(8) for x in range(4)] for z in range(8)] + [
    [device(y, x, 1, z) for z in range(8) for x in range(4)] for y in range(8)
]
LINES = [[device(y, x, 0, z) for z in range(8)] for y in range(8) for x in range(4)] + [
    [device(y, x, 1, z) for y in range(8)] for z in range(8) for x in range(4)
]


def reduce_over_devices(keep, send):
    half = keep + lax.ppermute(send, "c", [(0, 1), (1, 0)])
    mine = jnp.sum(lax.all_to_all(half, ALL, 0, 0, axis_index_groups=PLANES), axis=0)
    parts = lax.all_to_all(jnp.broadcast_to(mine[None], (8,) + mine.shape), ALL, 0, 0, axis_index_groups=LINES)
    return jnp.sum(parts, axis=0)


def spread(mine):
    copies = jnp.broadcast_to(mine[None], (PARTS,) + mine.shape)
    half = lax.all_to_all(copies, ALL, 0, 0, axis_index_groups=PLANES)
    half = half.reshape(-1, B)
    return half, lax.ppermute(half, "c", [(0, 1), (1, 0)])


def local(row_count, panel_block, trailing):
    core = lax.axis_index("c").astype(jnp.int32).reshape(1)
    mine = reduce_over_devices(*gram(core, panel_block, trailing))
    gm, go = spread(mine[:G_ROWS])
    cm, co = spread(mine[G_ROWS:])
    x, r = factor(row_count, core, gm, go)
    return r, update(row_count, core, x, cm, co, panel_block, trailing)


def solution(mesh):
    fine = Mesh(mesh.devices.reshape(8, 4, 2, 8), ("y", "x", "c", "z"))
    axes = ("y", "x", "c", "z")

    def run(panel_block, trailing):
        rows = panel_block.shape[0]
        f = jax.shard_map(
            lambda a, t: local(rows, a, t),
            mesh=fine,
            in_specs=(P(axes, None), P(axes, None)),
            out_specs=(P(), P(axes, None)),
            check_vma=False,
        )
        return f(panel_block, trailing)

    return run
```

```python
import jax
import jax.numpy as jnp
from jax import lax
from jax.experimental import pallas as pl
from jax.experimental.pallas import tpu as pltpu
from jax.sharding import Mesh, PartitionSpec as P

HI = lax.Precision.HIGHEST
B = 128
NP = 4
NC = 6
G_BLOCKS = [(i, j) for i in range(NP) for j in range(i, NP)]
C_BLOCKS = [(i, j) for i in range(NP) for j in range(NC)]
G_HALF = 6
C_HALF = 12
VM = pl.BlockSpec(memory_space=pltpu.VMEM)
SM = pl.BlockSpec(memory_space=pltpu.SMEM)


def split_half(blocks):
    n = (len(blocks) + 1) // 2
    return [(b, 0 if k < n else 1, k if k < n else k - n) for k, b in enumerate(blocks)]


PARTS = 32
ROOM = pltpu.CompilerParams(vmem_limit_bytes=20 << 20)
G_ROWS = G_HALF * B // PARTS
C_ROWS = C_HALF * B // PARTS


def gram_kernel(core_ref, a_ref, t_ref, keep_ref, send_ref):
    g_place = {b: (owner, slot) for b, owner, slot in split_half(G_BLOCKS)}
    c_place = {b: (owner, slot) for b, owner, slot in split_half(C_BLOCKS)}

    def put(ref, value, slot, start, rows):
        for p in range(0, B, 8):
            part, at = divmod(slot * B + p, rows)
            ref[part, start + at : start + at + 8, :] = value[p : p + 8]

    def fill(me):
        refs = (keep_ref, send_ref) if me == 0 else (send_ref, keep_ref)
        for i in range(NP):
            left = a_ref[:, i * B : (i + 1) * B]
            g = dot_t(left, a_ref[:, i * B :])
            for j in range(i, NP):
                owner, slot = g_place[(i, j)]
                put(refs[owner], g[:, (j - i) * B : (j - i + 1) * B], slot, 0, G_ROWS)
            c = dot_t(left, t_ref[...])
            for j in range(NC):
                owner, slot = c_place[(i, j)]
                put(refs[owner], c[:, j * B : (j + 1) * B], slot, G_ROWS, C_ROWS)
        for ref in refs:
            put(ref, jnp.zeros((B, B), jnp.float32), G_HALF - 1, 0, G_ROWS)

    for me in range(2):
        pl.when(core_ref[0] == me)(lambda me=me: fill(me))


def gram(core, a, t):
    out = jax.ShapeDtypeStruct((PARTS, G_ROWS + C_ROWS, B), jnp.float32)
    return pl.pallas_call(
        gram_kernel,
        out_shape=(out, out),
        in_specs=[SM, VM, VM],
        out_specs=[VM] * 2,
        cost_estimate=pl.CostEstimate(flops=2 * 192 * 512 * 1280, bytes_accessed=4 << 20, transcendentals=0),
        compiler_params=ROOM, name="gram",
    )(core, a, t)


def stack_pieces(u, order):
    high = u.astype(jnp.bfloat16).astype(jnp.float32)
    rest = u - high
    mid = rest.astype(jnp.bfloat16).astype(jnp.float32)
    part = (high, mid, rest - mid)
    return jnp.concatenate([part[k] for k in order], axis=0).astype(jnp.bfloat16)


LEFT = (0, 0, 1, 0, 2, 1)
RIGHT = (0, 1, 0, 2, 0, 1)


def row_of(v, t):
    return jnp.broadcast_to(v[t : t + 1, :], v.shape)


def eliminate_rows(w_rows, v_rows, base):
    sub = lax.broadcasted_iota(jnp.int32, (8, B), 0)
    d = {}
    for k in range(8):
        col = jnp.take_along_axis(w_rows, jnp.full((8, B), base + k, jnp.int32), axis=1, mode="promise_in_bounds")
        for i in range(k + 1):
            d[i, k] = row_of(col, i)
    w = [row_of(w_rows, t) for t in range(8)]
    v = [row_of(v_rows, t) for t in range(8)]
    for t in range(8):
        inv = lax.rsqrt(d[t, t])
        u = {k: d[t, k] * inv for k in range(t + 1, 8)}
        for i in range(t + 1, 8):
            for k in range(i, 8):
                d[i, k] = d[i, k] - u[i] * u[k]
        w[t] = w[t] * inv
        v[t] = v[t] * inv
        for i in range(t + 1, 8):
            w[i] = w[i] - u[i] * w[t]
            v[i] = v[i] - u[i] * v[t]
    wo, vo = w[0], v[0]
    for t in range(1, 8):
        wo = jnp.where(sub == t, w[t], wo)
        vo = jnp.where(sub == t, v[t], vo)
    return wo, vo


def diag_factor(s, e, rkk):
    lane = lax.broadcasted_iota(jnp.int32, (8, B), 1)
    sub = lax.broadcasted_iota(jnp.int32, (8, B), 0)
    e[...] = jnp.where(
        lax.broadcasted_iota(jnp.int32, (B, B), 0) == lax.broadcasted_iota(jnp.int32, (B, B), 1), 1.0, 0.0
    ).astype(jnp.float32)

    def body(g, _):
        base = pl.multiple_of(g * 8, 8)
        rows = pl.ds(base, 8)
        u, v = eliminate_rows(s[rows, :], e[rows, :], base)
        rkk[rows, :] = jnp.where(lane >= sub + base, u, 0.0)
        left = stack_pieces(jnp.where(lane >= base + 8, u, 0.0), LEFT)
        right = jnp.concatenate([stack_pieces(u, RIGHT), stack_pieces(v, RIGHT)], axis=1)
        change = lax.dot_general(left, right, (((0,), (0,)), ((), ())), preferred_element_type=jnp.float32)
        s[...] = s[...] - change[:, :B]
        e[...] = e[...] - change[:, B:]
        e[rows, :] = v
        return 0

    lax.fori_loop(0, B // 8, body, 0)


def dot(x, y):
    return jnp.dot(x, y, precision=HI, preferred_element_type=jnp.float32)


def dot_t(x, y):
    return lax.dot_general(x, y, (((0,), (0,)), ((), ())), precision=HI, preferred_element_type=jnp.float32)


def panel_step(k, x, rkk, s, lkk):
    r0 = k * B
    r1 = r0 + B
    s[...] = x[r0:r1, r0:r1]
    diag_factor(s, lkk, rkk)
    linv = lkk[...]
    if k > 0:
        x[r0:r1, :r0] = dot(linv, x[r0:r1, :r0])
    if k < NP - 1:
        x[r0:r1, r1:] = dot(linv, x[r0:r1, r1:])
    x[r0:r1, r0:r1] = linv
    for i in range(k + 1, NP):
        c0 = i * B
        left = x[r0:r1, c0 : c0 + B]
        x[c0 : c0 + B, c0:] = x[c0 : c0 + B, c0:] - dot_t(left, x[r0:r1, c0:])
        low = dot_t(left, x[r0:r1, :r1])
        if k > 0:
            x[c0 : c0 + B, :r0] = x[c0 : c0 + B, :r0] - low[:, :r0]
        x[c0 : c0 + B, r0:r1] = -low[:, r0:]


LAST = NP - 1


def first_kernel(row_count, core_ref, gm_ref, go_ref, x_ref, d_ref, s, lkk):
    scale = 1.0 / row_count
    for me in range(2):

        @pl.when(core_ref[0] == me)
        def _(me=me):
            refs = (gm_ref, go_ref) if me == 0 else (go_ref, gm_ref)
            for (i, j), owner, slot in split_half(G_BLOCKS):
                x_ref[i * B : (i + 1) * B, j * B : (j + 1) * B] = refs[owner][slot * B : (slot + 1) * B, :] * scale

    for i in range(NP):
        for j in range(i):
            x_ref[i * B : (i + 1) * B, j * B : (j + 1) * B] = jnp.zeros((B, B), jnp.float32)
    for k in range(LAST):
        panel_step(k, x_ref, d_ref.at[pl.ds(k * B, B), :], s, lkk)


def last_kernel(xi_ref, d_ref, li_ref, r_ref, rkk, s, lkk):
    r0 = LAST * B
    for i in range(LAST):
        rows = slice(i * B, (i + 1) * B)
        r_ref[rows, :] = xi_ref[rows, :]
        r_ref[rows, rows] = d_ref[rows, :]
        if i > 0:
            r_ref[rows, : i * B] = jnp.zeros((B, i * B), jnp.float32)
    li_ref[...] = xi_ref[...]
    panel_step(LAST, li_ref, rkk, s, lkk)
    r_ref[r0:, :r0] = jnp.zeros((B, r0), jnp.float32)
    r_ref[r0:, r0:] = rkk[...]
    for i in (0, 2):
        li_ref[i * B : (i + 1) * B, (i + 1) * B : (i + 2) * B] = jnp.zeros((B, B), jnp.float32)


def factor(row_count, core, gm, go):
    full = jax.ShapeDtypeStruct((NP * B, NP * B), jnp.float32)
    scratch = pltpu.VMEM((B, B), jnp.float32)
    cost = pl.CostEstimate(flops=4_000_000_000, bytes_accessed=2 << 20, transcendentals=0)
    x, d = pl.pallas_call(
        lambda *refs: first_kernel(row_count, *refs),
        out_shape=(full, jax.ShapeDtypeStruct((LAST * B, B), jnp.float32)), in_specs=[SM, VM, VM], out_specs=[VM, VM],
        scratch_shapes=[scratch] * 2, cost_estimate=cost, compiler_params=ROOM, name="factor0",
    )(core, gm, go)
    return pl.pallas_call(
        last_kernel,
        out_shape=(full, full), in_specs=[VM] * 2, out_specs=[VM, VM],
        scratch_shapes=[scratch] * 3, cost_estimate=cost, compiler_params=ROOM, name="factor3",
    )(x, d)


def update_kernel(row_count, core_ref, x_ref, cm_ref, co_ref, a_ref, t_ref, out_ref, c, q, p):
    scale = 1.0 / row_count
    h = NP * B // 2
    for me in range(2):

        @pl.when(core_ref[0] == me)
        def _(me=me):
            refs = (cm_ref, co_ref) if me == 0 else (co_ref, cm_ref)
            for (i, j), owner, slot in split_half(C_BLOCKS):
                c[i * B : (i + 1) * B, j * B : (j + 1) * B] = refs[owner][slot * B : (slot + 1) * B, :] * scale

    for r0 in (0, h):
        r1 = r0 + h
        q[:, r0:r1] = lax.dot_general(
            a_ref[:, :r1], x_ref[r0:r1, :r1], (((1,), (1,)), ((), ())), precision=HI, preferred_element_type=jnp.float32
        )
        p[r0:r1, :] = dot(x_ref[r0:r1, :r1], c[:r1, :])
    out_ref[...] = t_ref[...] - dot(q[...], p[...])


def update(row_count, core, x, cm, co, a, t):
    wide = pltpu.VMEM((NP * B, NC * B), jnp.float32)
    return pl.pallas_call(
        lambda *refs: update_kernel(row_count, *refs),
        out_shape=jax.ShapeDtypeStruct(t.shape, jnp.float32),
        in_specs=[SM] + [VM] * 5, out_specs=VM,
        scratch_shapes=[wide, pltpu.VMEM(a.shape, jnp.float32), wide],
        cost_estimate=pl.CostEstimate(flops=4_000_000_000, bytes_accessed=4 << 20, transcendentals=0), compiler_params=ROOM, name="update",
    )(core, x, cm, co, a, t)


ALL = ("y", "x", "c", "z")


def device(y, x, c, z):
    return ((y * 4 + x) * 2 + c) * 8 + z


PLANES = [[device(y, x, 0, z) for y in range(8) for x in range(4)] for z in range(8)] + [
    [device(y, x, 1, z) for z in range(8) for x in range(4)] for y in range(8)
]
LINES = [[device(y, x, 0, z) for z in range(8)] for y in range(8) for x in range(4)] + [
    [device(y, x, 1, z) for y in range(8)] for z in range(8) for x in range(4)
]


def reduce_over_devices(keep, send):
    half = keep + lax.ppermute(send, "c", [(0, 1), (1, 0)])
    mine = jnp.sum(lax.all_to_all(half, ALL, 0, 0, axis_index_groups=PLANES), axis=0)
    parts = lax.all_to_all(jnp.broadcast_to(mine[None], (8,) + mine.shape), ALL, 0, 0, axis_index_groups=LINES)
    return jnp.sum(parts, axis=0)


def spread(mine):
    copies = jnp.broadcast_to(mine[None], (PARTS,) + mine.shape)
    half = lax.all_to_all(copies, ALL, 0, 0, axis_index_groups=PLANES)
    half = half.reshape(-1, B)
    return half, lax.ppermute(half, "c", [(0, 1), (1, 0)])


def local(row_count, panel_block, trailing):
    core = lax.axis_index("c").astype(jnp.int32).reshape(1)
    mine = reduce_over_devices(*gram(core, panel_block, trailing))
    gm, go = spread(mine[:G_ROWS])
    cm, co = spread(mine[G_ROWS:])
    x, r = factor(row_count, core, gm, go)
    return r, update(row_count, core, x, cm, co, panel_block, trailing)


def solution(mesh):
    fine = Mesh(mesh.devices.reshape(8, 4, 2, 8), ("y", "x", "c", "z"))
    axes = ("y", "x", "c", "z")

    def run(panel_block, trailing):
        rows = panel_block.shape[0]
        f = jax.shard_map(
            lambda a, t: local(rows, a, t),
            mesh=fine,
            in_specs=(P(axes, None), P(axes, None)),
            out_specs=(P(), P(axes, None)),
            check_vma=False,
        )
        return f(panel_block, trailing)

    return run
```

```python
import jax
import jax.numpy as jnp
from jax import lax
from jax.experimental import pallas as pl
from jax.experimental.pallas import tpu as pltpu
from jax.sharding import Mesh, PartitionSpec as P

HI = lax.Precision.HIGHEST
B = 128
NP = 4
NC = 6
G_BLOCKS = [(i, j) for i in range(NP) for j in range(i, NP)]
C_BLOCKS = [(i, j) for i in range(NP) for j in range(NC)]
G_HALF = 6
C_HALF = 12
VM = pl.BlockSpec(memory_space=pltpu.VMEM)
SM = pl.BlockSpec(memory_space=pltpu.SMEM)


def split_half(blocks):
    n = (len(blocks) + 1) // 2
    return [(b, 0 if k < n else 1, k if k < n else k - n) for k, b in enumerate(blocks)]


PARTS = 32
ROOM = pltpu.CompilerParams(vmem_limit_bytes=20 << 20)
G_ROWS = G_HALF * B // PARTS
C_ROWS = C_HALF * B // PARTS


def products(mine, core, a_ref, t_ref, out_ref, ready):
    g_place = {b: (owner, slot) for b, owner, slot in split_half(G_BLOCKS)}
    c_place = {b: (owner, slot) for b, owner, slot in split_half(C_BLOCKS)}

    def put(value, slot, start, rows):
        for p in range(0, B, 8):
            part, at = divmod(slot * B + p, rows)
            out_ref[part, start + at : start + at + 8, :] = value[p : p + 8]

    def fill(me):
        owner = me if mine else 1 - me
        ready(0)
        for i in range(NP):
            cols = [j for j in range(i, NP) if g_place[(i, j)][0] == owner]
            if cols:
                lo, hi = min(cols), max(cols) + 1
                g = dot_t(a_ref[:, i * B : (i + 1) * B], a_ref[:, lo * B : hi * B])
                for j in cols:
                    put(g[:, (j - lo) * B : (j - lo + 1) * B], g_place[(i, j)][1], 0, G_ROWS)
        put(jnp.zeros((B, B), jnp.float32), G_HALF - 1, 0, G_ROWS)
        ready(1)
        for i in range(NP):
            cols = [j for j in range(NC) if c_place[(i, j)][0] == owner]
            if cols:
                lo, hi = min(cols), max(cols) + 1
                c = dot_t(a_ref[:, i * B : (i + 1) * B], t_ref[:, lo * B : hi * B])
                for j in cols:
                    put(c[:, (j - lo) * B : (j - lo + 1) * B], c_place[(i, j)][1], G_ROWS, C_ROWS)

    for me in range(2):
        pl.when(core == me)(lambda me=me: fill(me))


def send_kernel(core_ref, a_hbm, t_hbm, out_ref, a_ref, t_ref, sem):
    copies = [pltpu.make_async_copy(a_hbm, a_ref, sem.at[0]), pltpu.make_async_copy(t_hbm, t_ref, sem.at[1])]
    for copy in copies:
        copy.start()
    products(False, core_ref[0], a_ref, t_ref, out_ref, lambda k: copies[k].wait())


def keep_kernel(core_ref, a_ref, t_ref, out_ref):
    products(True, core_ref[0], a_ref, t_ref, out_ref, lambda k: None)


def gram(core, a, t):
    out = jax.ShapeDtypeStruct((PARTS, G_ROWS + C_ROWS, B), jnp.float32)
    cost = pl.CostEstimate(flops=192 * 512 * 1280, bytes_accessed=2 << 20, transcendentals=0)
    hbm = pl.BlockSpec(memory_space=pltpu.HBM)
    send = pl.pallas_call(
        send_kernel,
        out_shape=out, in_specs=[SM, hbm, hbm], out_specs=VM,
        scratch_shapes=[pltpu.VMEM(a.shape, a.dtype), pltpu.VMEM(t.shape, t.dtype), pltpu.SemaphoreType.DMA((2,))],
        cost_estimate=cost, name="gram_send",
    )(core, a, t)
    keep = pl.pallas_call(
        keep_kernel,
        out_shape=out, in_specs=[SM, VM, VM], out_specs=VM,
        compiler_params=ROOM, cost_estimate=cost, name="gram_keep",
    )(core, a, t)
    return keep, send


def stack_pieces(u, order):
    high = u.astype(jnp.bfloat16).astype(jnp.float32)
    rest = u - high
    mid = rest.astype(jnp.bfloat16).astype(jnp.float32)
    part = (high, mid, rest - mid)
    return jnp.concatenate([part[k] for k in order], axis=0).astype(jnp.bfloat16)


LEFT = (0, 0, 1, 0, 2, 1)
RIGHT = (0, 1, 0, 2, 0, 1)


def row_of(v, t):
    return jnp.broadcast_to(v[t : t + 1, :], v.shape)


def lane_of(v, index):
    return jnp.take_along_axis(v, index, axis=1, mode="promise_in_bounds")


def eliminate(w_rows, v_rows, w_next, v_next, base):
    sub = lax.broadcasted_iota(jnp.int32, (8, B), 0)
    ahead = jnp.minimum(base + 8 + sub, B - 1)
    d = {}
    for k in range(8):
        col = lane_of(w_rows, jnp.full((8, B), base + k, jnp.int32))
        for i in range(k + 1):
            d[i, k] = row_of(col, i)
    w = [row_of(w_rows, t) for t in range(8)]
    v = [row_of(v_rows, t) for t in range(8)]
    for t in range(8):
        inv = lax.rsqrt(d[t, t])
        u = {k: d[t, k] * inv for k in range(t + 1, 8)}
        for i in range(t + 1, 8):
            for k in range(i, 8):
                d[i, k] = d[i, k] - u[i] * u[k]
        w[t] = w[t] * inv
        v[t] = v[t] * inv
        for i in range(t + 1, 8):
            w[i] = w[i] - u[i] * w[t]
            v[i] = v[i] - u[i] * v[t]
        weight = lane_of(w[t], ahead)
        w_next = w_next - weight * w[t]
        v_next = v_next - weight * v[t]
    wo, vo = w[0], v[0]
    for t in range(1, 8):
        wo = jnp.where(sub == t, w[t], wo)
        vo = jnp.where(sub == t, v[t], vo)
    return wo, vo, w_next, v_next


def apply_rows(w, v, w_next, v_next, base):
    sub = lax.broadcasted_iota(jnp.int32, (8, B), 0)
    ahead = jnp.minimum(base + 8 + sub, B - 1)
    for t in range(8):
        row = row_of(w, t)
        weight = lane_of(row, ahead)
        w_next = w_next - weight * row
        v_next = v_next - weight * row_of(v, t)
    return w_next, v_next


def diag_factor(s, e, rkk, lkk):
    lane = lax.broadcasted_iota(jnp.int32, (8, B), 1)
    sub = lax.broadcasted_iota(jnp.int32, (8, B), 0)
    zero = jnp.zeros((8, B), jnp.float32)
    e[:B, :] = jnp.where(
        lax.broadcasted_iota(jnp.int32, (B, B), 0) == lax.broadcasted_iota(jnp.int32, (B, B), 1), 1.0, 0.0
    ).astype(jnp.float32)
    s[B:, :] = zero
    e[B:, :] = zero

    def body(g, carry):
        w, v, w_last, v_last = carry
        base = pl.multiple_of(g * 8, 8)
        rows = pl.ds(base, 8)
        after = pl.ds(base + 8, 8)
        left = stack_pieces(w_last, LEFT)
        right = jnp.concatenate([stack_pieces(w_last, RIGHT), stack_pieces(v_last, RIGHT)], axis=1)
        change = lax.dot_general(left, right, (((0,), (0,)), ((), ())), preferred_element_type=jnp.float32)
        w_next, v_next = apply_rows(w_last, v_last, s[after, :], e[after, :], base)
        w, v, w_next, v_next = eliminate(w, v, w_next, v_next, base)
        rkk[rows, :] = jnp.where(lane >= sub + base, w, 0.0)
        lkk[rows, :] = v
        s[:B, :] = s[:B, :] - change[:, :B]
        e[:B, :] = e[:B, :] - change[:, B:]
        return w_next, v_next, w, v

    lax.fori_loop(0, B // 8, body, (s[:8, :], e[:8, :], zero, zero))


def dot(x, y):
    return jnp.dot(x, y, precision=HI, preferred_element_type=jnp.float32)


def dot_t(x, y):
    return lax.dot_general(x, y, (((0,), (0,)), ((), ())), precision=HI, preferred_element_type=jnp.float32)


def panel_step(k, x, rkk, s, e, lkk):
    r0 = k * B
    r1 = r0 + B
    s[:B, :] = x[r0:r1, r0:r1]
    diag_factor(s, e, rkk, lkk)
    linv = lkk[...]
    if k == NP - 1:
        x[r0:, :r0] = dot(linv, x[r0:, :r0])
    else:
        x[r0:r1, :] = dot(linv, x[r0:r1, :])
    x[r0:r1, r0:r1] = linv
    if k < NP - 1:
        change = dot_t(x[r0:r1, r1:], x[r0:r1, :])
        for i in range(k + 1, NP):
            c0 = i * B
            part = change[c0 - r1 : c0 - r1 + B]
            x[c0 : c0 + B, c0:] = x[c0 : c0 + B, c0:] - part[:, c0:]
            if k > 0:
                x[c0 : c0 + B, :r0] = x[c0 : c0 + B, :r0] - part[:, :r0]
            x[c0 : c0 + B, r0:r1] = -part[:, r0:r1]


LAST = NP - 1


def first_kernel(row_count, core_ref, gm_ref, go_ref, x_ref, d_ref, s, e, lkk):
    scale = 1.0 / row_count
    for me in range(2):

        @pl.when(core_ref[0] == me)
        def _(me=me):
            refs = (gm_ref, go_ref) if me == 0 else (go_ref, gm_ref)
            for (i, j), owner, slot in split_half(G_BLOCKS):
                x_ref[i * B : (i + 1) * B, j * B : (j + 1) * B] = refs[owner][slot * B : (slot + 1) * B, :] * scale

    for i in range(NP):
        for j in range(i):
            x_ref[i * B : (i + 1) * B, j * B : (j + 1) * B] = jnp.zeros((B, B), jnp.float32)
    for k in range(LAST):
        panel_step(k, x_ref, d_ref.at[pl.ds(k * B, B), :], s, e, lkk)


def last_kernel(xi_ref, d_ref, li_ref, r_ref, s, e, lkk, rkk):
    r0 = LAST * B
    for i in range(LAST):
        rows = slice(i * B, (i + 1) * B)
        r_ref[rows, :] = xi_ref[rows, :]
        r_ref[rows, rows] = d_ref[rows, :]
        if i > 0:
            r_ref[rows, : i * B] = jnp.zeros((B, i * B), jnp.float32)
    li_ref[...] = xi_ref[...]
    panel_step(LAST, li_ref, rkk, s, e, lkk)
    r_ref[r0:, :r0] = jnp.zeros((B, r0), jnp.float32)
    r_ref[r0:, r0:] = rkk[...]
    for i in (0, 2):
        li_ref[i * B : (i + 1) * B, (i + 1) * B : (i + 2) * B] = jnp.zeros((B, B), jnp.float32)


def factor(row_count, core, gm, go):
    full = jax.ShapeDtypeStruct((NP * B, NP * B), jnp.float32)
    work = [pltpu.VMEM((B + 8, B), jnp.float32)] * 2 + [pltpu.VMEM((B, B), jnp.float32)]
    cost = pl.CostEstimate(flops=4_000_000_000, bytes_accessed=2 << 20, transcendentals=0)
    x, d = pl.pallas_call(
        lambda *refs: first_kernel(row_count, *refs),
        out_shape=(full, jax.ShapeDtypeStruct((LAST * B, B), jnp.float32)), in_specs=[SM, VM, VM], out_specs=[VM, VM],
        scratch_shapes=work, cost_estimate=cost, compiler_params=ROOM, name="factor0",
    )(core, gm, go)
    return pl.pallas_call(
        last_kernel,
        out_shape=(full, full), in_specs=[VM] * 2, out_specs=[VM, VM],
        scratch_shapes=work + [pltpu.VMEM((B, B), jnp.float32)], cost_estimate=cost, compiler_params=ROOM, name="factor3",
    )(x, d)


def update_kernel(row_count, core_ref, x_ref, cm_ref, co_ref, a_ref, t_ref, out_ref, c, q, p):
    scale = 1.0 / row_count
    h = NP * B // 2
    for me in range(2):

        @pl.when(core_ref[0] == me)
        def _(me=me):
            refs = (cm_ref, co_ref) if me == 0 else (co_ref, cm_ref)
            for (i, j), owner, slot in split_half(C_BLOCKS):
                c[i * B : (i + 1) * B, j * B : (j + 1) * B] = refs[owner][slot * B : (slot + 1) * B, :] * scale

    for r0 in (0, h):
        r1 = r0 + h
        q[:, r0:r1] = lax.dot_general(
            a_ref[:, :r1], x_ref[r0:r1, :r1], (((1,), (1,)), ((), ())), precision=HI, preferred_element_type=jnp.float32
        )
        p[r0:r1, :] = dot(x_ref[r0:r1, :r1], c[:r1, :])
    out_ref[...] = t_ref[...] - dot(q[...], p[...])


def update(row_count, core, x, cm, co, a, t):
    wide = pltpu.VMEM((NP * B, NC * B), jnp.float32)
    return pl.pallas_call(
        lambda *refs: update_kernel(row_count, *refs),
        out_shape=jax.ShapeDtypeStruct(t.shape, jnp.float32),
        in_specs=[SM] + [VM] * 5, out_specs=VM,
        scratch_shapes=[wide, pltpu.VMEM(a.shape, jnp.float32), wide],
        cost_estimate=pl.CostEstimate(flops=4_000_000_000, bytes_accessed=4 << 20, transcendentals=0), compiler_params=ROOM, name="update",
    )(core, x, cm, co, a, t)


ALL = ("y", "x", "c", "z")


def device(y, x, c, z):
    return ((y * 4 + x) * 2 + c) * 8 + z


PLANES = [[device(y, x, 0, z) for y in range(8) for x in range(4)] for z in range(8)] + [
    [device(y, x, 1, z) for z in range(8) for x in range(4)] for y in range(8)
]
LINES = [[device(y, x, 0, z) for z in range(8)] for y in range(8) for x in range(4)] + [
    [device(y, x, 1, z) for y in range(8)] for z in range(8) for x in range(4)
]


def reduce_over_devices(keep, send):
    half = keep + lax.ppermute(send, "c", [(0, 1), (1, 0)])
    mine = jnp.sum(lax.all_to_all(half, ALL, 0, 0, axis_index_groups=PLANES), axis=0)
    parts = lax.all_to_all(jnp.broadcast_to(mine[None], (8,) + mine.shape), ALL, 0, 0, axis_index_groups=LINES)
    return jnp.sum(parts, axis=0)


def spread(mine):
    copies = jnp.broadcast_to(mine[None], (PARTS,) + mine.shape)
    half = lax.all_to_all(copies, ALL, 0, 0, axis_index_groups=PLANES)
    half = half.reshape(-1, B)
    return half, lax.ppermute(half, "c", [(0, 1), (1, 0)])


def local(row_count, panel_block, trailing):
    core = lax.axis_index("c").astype(jnp.int32).reshape(1)
    mine = reduce_over_devices(*gram(core, panel_block, trailing))
    mine_g, mine_c = lax.optimization_barrier((mine[:G_ROWS], mine[G_ROWS:]))
    gm, go = spread(mine_g)
    cm, co = spread(mine_c)
    x, r = factor(row_count, core, gm, go)
    return r, update(row_count, core, x, cm, co, panel_block, trailing)


def solution(mesh):
    fine = Mesh(mesh.devices.reshape(8, 4, 2, 8), ("y", "x", "c", "z"))
    axes = ("y", "x", "c", "z")

    def run(panel_block, trailing):
        rows = panel_block.shape[0]
        f = jax.shard_map(
            lambda a, t: local(rows, a, t),
            mesh=fine,
            in_specs=(P(axes, None), P(axes, None)),
            out_specs=(P(), P(axes, None)),
            check_vma=False,
        )
        return f(panel_block, trailing)

    return run
```

```python
import jax
import jax.numpy as jnp
from jax import lax
from jax.experimental import pallas as pl
from jax.experimental.pallas import tpu as pltpu
from jax.sharding import Mesh, PartitionSpec as P

HI = lax.Precision.HIGHEST
B = 128
NP = 4
NC = 6
G_BLOCKS = [(i, j) for i in range(NP) for j in range(i, NP)]
C_BLOCKS = [(i, j) for i in range(NP) for j in range(NC)]
G_HALF = 6
C_HALF = 12
VM = pl.BlockSpec(memory_space=pltpu.VMEM)
SM = pl.BlockSpec(memory_space=pltpu.SMEM)


def split_half(blocks):
    n = (len(blocks) + 1) // 2
    return [(b, 0 if k < n else 1, k if k < n else k - n) for k, b in enumerate(blocks)]


PARTS = 32
ROOM = pltpu.CompilerParams(vmem_limit_bytes=20 << 20)
G_ROWS = G_HALF * B // PARTS
C_ROWS = C_HALF * B // PARTS


def products(mine, core, a_ref, t_ref, out_ref, ready):
    g_place = {b: (owner, slot) for b, owner, slot in split_half(G_BLOCKS)}
    c_place = {b: (owner, slot) for b, owner, slot in split_half(C_BLOCKS)}

    def put(value, slot, start, rows):
        for p in range(0, B, 8):
            part, at = divmod(slot * B + p, rows)
            out_ref[part, start + at : start + at + 8, :] = value[p : p + 8]

    def fill(me):
        owner = me if mine else 1 - me
        ready(0)
        for i in range(NP):
            cols = [j for j in range(i, NP) if g_place[(i, j)][0] == owner]
            if cols:
                lo, hi = min(cols), max(cols) + 1
                g = dot_t(a_ref[:, i * B : (i + 1) * B], a_ref[:, lo * B : hi * B])
                for j in cols:
                    put(g[:, (j - lo) * B : (j - lo + 1) * B], g_place[(i, j)][1], 0, G_ROWS)
        put(jnp.zeros((B, B), jnp.float32), G_HALF - 1, 0, G_ROWS)
        ready(1)
        for i in range(NP):
            cols = [j for j in range(NC) if c_place[(i, j)][0] == owner]
            if cols:
                lo, hi = min(cols), max(cols) + 1
                c = dot_t(a_ref[:, i * B : (i + 1) * B], t_ref[:, lo * B : hi * B])
                for j in cols:
                    put(c[:, (j - lo) * B : (j - lo + 1) * B], c_place[(i, j)][1], G_ROWS, C_ROWS)

    for me in range(2):
        pl.when(core == me)(lambda me=me: fill(me))


def send_kernel(core_ref, a_hbm, t_hbm, out_ref, a_ref, t_ref, sem):
    copies = [pltpu.make_async_copy(a_hbm, a_ref, sem.at[0]), pltpu.make_async_copy(t_hbm, t_ref, sem.at[1])]
    for copy in copies:
        copy.start()
    products(False, core_ref[0], a_ref, t_ref, out_ref, lambda k: copies[k].wait())


def keep_kernel(core_ref, a_ref, t_ref, out_ref):
    products(True, core_ref[0], a_ref, t_ref, out_ref, lambda k: None)


def gram(core, a, t):
    out = jax.ShapeDtypeStruct((PARTS, G_ROWS + C_ROWS, B), jnp.float32)
    cost = pl.CostEstimate(flops=192 * 512 * 1280, bytes_accessed=2 << 20, transcendentals=0)
    hbm = pl.BlockSpec(memory_space=pltpu.HBM)
    send = pl.pallas_call(
        send_kernel,
        out_shape=out, in_specs=[SM, hbm, hbm], out_specs=VM,
        scratch_shapes=[pltpu.VMEM(a.shape, a.dtype), pltpu.VMEM(t.shape, t.dtype), pltpu.SemaphoreType.DMA((2,))],
        cost_estimate=cost, name="gram_send",
    )(core, a, t)
    keep = pl.pallas_call(
        keep_kernel,
        out_shape=out, in_specs=[SM, VM, VM], out_specs=VM,
        cost_estimate=cost, name="gram_keep",
    )(core, a, t)
    return keep, send


def stack_pieces(u, order):
    high = u.astype(jnp.bfloat16).astype(jnp.float32)
    rest = u - high
    mid = rest.astype(jnp.bfloat16).astype(jnp.float32)
    part = (high, mid, rest - mid)
    return jnp.concatenate([part[k] for k in order], axis=0).astype(jnp.bfloat16)


LEFT = (0, 0, 1, 0, 2, 1)
RIGHT = (0, 1, 0, 2, 0, 1)


def row_of(v, t):
    return jnp.broadcast_to(v[t : t + 1, :], v.shape)


def lane_of(v, index):
    return jnp.take_along_axis(v, index, axis=1, mode="promise_in_bounds")


def eliminate(w_rows, v_rows, w_next, v_next, base):
    sub = lax.broadcasted_iota(jnp.int32, (8, B), 0)
    ahead = jnp.minimum(base + 8 + sub, B - 1)
    d = {}
    for k in range(8):
        col = lane_of(w_rows, jnp.full((8, B), base + k, jnp.int32))
        for i in range(k + 1):
            d[i, k] = row_of(col, i)
    w = [row_of(w_rows, t) for t in range(8)]
    v = [row_of(v_rows, t) for t in range(8)]
    for t in range(8):
        inv = lax.rsqrt(d[t, t])
        u = {k: d[t, k] * inv for k in range(t + 1, 8)}
        for i in range(t + 1, 8):
            for k in range(i, 8):
                d[i, k] = d[i, k] - u[i] * u[k]
        w[t] = w[t] * inv
        v[t] = v[t] * inv
        for i in range(t + 1, 8):
            w[i] = w[i] - u[i] * w[t]
            v[i] = v[i] - u[i] * v[t]
        weight = lane_of(w[t], ahead)
        w_next = w_next - weight * w[t]
        v_next = v_next - weight * v[t]
    wo, vo = w[0], v[0]
    for t in range(1, 8):
        wo = jnp.where(sub == t, w[t], wo)
        vo = jnp.where(sub == t, v[t], vo)
    return wo, vo, w_next, v_next


def apply_rows(w, v, w_next, v_next, base):
    sub = lax.broadcasted_iota(jnp.int32, (8, B), 0)
    ahead = jnp.minimum(base + 8 + sub, B - 1)
    for t in range(8):
        row = row_of(w, t)
        weight = lane_of(row, ahead)
        w_next = w_next - weight * row
        v_next = v_next - weight * row_of(v, t)
    return w_next, v_next


def diag_factor(s, e, rkk, lkk):
    lane = lax.broadcasted_iota(jnp.int32, (8, B), 1)
    sub = lax.broadcasted_iota(jnp.int32, (8, B), 0)
    zero = jnp.zeros((8, B), jnp.float32)
    e[:B, :] = jnp.where(
        lax.broadcasted_iota(jnp.int32, (B, B), 0) == lax.broadcasted_iota(jnp.int32, (B, B), 1), 1.0, 0.0
    ).astype(jnp.float32)
    s[B:, :] = zero
    e[B:, :] = zero

    def body(g, carry):
        w, v, w_last, v_last = carry
        base = pl.multiple_of(g * 8, 8)
        rows = pl.ds(base, 8)
        after = pl.ds(base + 8, 8)
        left = stack_pieces(w_last, LEFT)
        right = jnp.concatenate([stack_pieces(w_last, RIGHT), stack_pieces(v_last, RIGHT)], axis=1)
        change = lax.dot_general(left, right, (((0,), (0,)), ((), ())), preferred_element_type=jnp.float32)
        w_next, v_next = apply_rows(w_last, v_last, s[after, :], e[after, :], base)
        w, v, w_next, v_next = eliminate(w, v, w_next, v_next, base)
        rkk[rows, :] = jnp.where(lane >= sub + base, w, 0.0)
        lkk[rows, :] = v
        s[:B, :] = s[:B, :] - change[:, :B]
        e[:B, :] = e[:B, :] - change[:, B:]
        return w_next, v_next, w, v

    lax.fori_loop(0, B // 8, body, (s[:8, :], e[:8, :], zero, zero))


def dot(x, y):
    return jnp.dot(x, y, precision=HI, preferred_element_type=jnp.float32)


def dot_t(x, y):
    return lax.dot_general(x, y, (((0,), (0,)), ((), ())), precision=HI, preferred_element_type=jnp.float32)


def panel_step(k, x, rkk, s, e, lkk):
    r0 = k * B
    r1 = r0 + B
    s[:B, :] = x[r0:r1, r0:r1]
    diag_factor(s, e, rkk, lkk)
    linv = lkk[...]
    if k == NP - 1:
        x[r0:, :r0] = dot(linv, x[r0:, :r0])
    else:
        x[r0:r1, :] = dot(linv, x[r0:r1, :])
    x[r0:r1, r0:r1] = linv
    if k < NP - 1:
        change = dot_t(x[r0:r1, r1:], x[r0:r1, :])
        for i in range(k + 1, NP):
            c0 = i * B
            part = change[c0 - r1 : c0 - r1 + B]
            x[c0 : c0 + B, c0:] = x[c0 : c0 + B, c0:] - part[:, c0:]
            if k > 0:
                x[c0 : c0 + B, :r0] = x[c0 : c0 + B, :r0] - part[:, :r0]
            x[c0 : c0 + B, r0:r1] = -part[:, r0:r1]


def factor_kernel(row_count, core_ref, gm_ref, go_ref, x_ref, r_ref, s, e, lkk):
    scale = 1.0 / row_count
    for me in range(2):

        @pl.when(core_ref[0] == me)
        def _(me=me):
            refs = (gm_ref, go_ref) if me == 0 else (go_ref, gm_ref)
            for (i, j), owner, slot in split_half(G_BLOCKS):
                x_ref[i * B : (i + 1) * B, j * B : (j + 1) * B] = refs[owner][slot * B : (slot + 1) * B, :] * scale

    for i in range(NP):
        rows = slice(i * B, (i + 1) * B)
        if i > 0:
            x_ref[rows, : i * B] = jnp.zeros((B, i * B), jnp.float32)
            r_ref[rows, : i * B] = jnp.zeros((B, i * B), jnp.float32)
    for k in range(NP):
        r0, r1 = k * B, (k + 1) * B
        panel_step(k, x_ref, r_ref.at[pl.ds(r0, B), pl.ds(r0, B)], s, e, lkk)
        if r1 < NP * B:
            r_ref[r0:r1, r1:] = x_ref[r0:r1, r1:]
    for i in (0, 2):
        x_ref[i * B : (i + 1) * B, (i + 1) * B : (i + 2) * B] = jnp.zeros((B, B), jnp.float32)


def factor(row_count, core, gm, go):
    full = jax.ShapeDtypeStruct((NP * B, NP * B), jnp.float32)
    return pl.pallas_call(
        lambda *refs: factor_kernel(row_count, *refs),
        out_shape=(full, full), in_specs=[SM, VM, VM], out_specs=[VM, VM],
        scratch_shapes=[pltpu.VMEM((B + 8, B), jnp.float32)] * 2 + [pltpu.VMEM((B, B), jnp.float32)],
        cost_estimate=pl.CostEstimate(flops=8_000_000_000, bytes_accessed=2 << 20, transcendentals=0),
        compiler_params=ROOM, name="factor",
    )(core, gm, go)


HALF = NP * B // 2


def basis_kernel(x_ref, a_ref, q_ref):
    for r0 in (0, HALF):
        r1 = r0 + HALF
        q_ref[:, r0:r1] = lax.dot_general(
            a_ref[:, :r1], x_ref[r0:r1, :r1], (((1,), (1,)), ((), ())), precision=HI, preferred_element_type=jnp.float32
        )


def basis(x, a):
    return pl.pallas_call(
        basis_kernel,
        out_shape=jax.ShapeDtypeStruct(a.shape, jnp.float32), in_specs=[VM, VM], out_specs=VM,
        cost_estimate=pl.CostEstimate(flops=1_000_000_000, bytes_accessed=2 << 20, transcendentals=0),
        compiler_params=ROOM, name="basis",
    )(x, a)


def update_kernel(row_count, core_ref, x_ref, cm_ref, co_ref, q_ref, t_ref, out_ref, c, p):
    scale = 1.0 / row_count
    for me in range(2):

        @pl.when(core_ref[0] == me)
        def _(me=me):
            refs = (cm_ref, co_ref) if me == 0 else (co_ref, cm_ref)
            for (i, j), owner, slot in split_half(C_BLOCKS):
                c[i * B : (i + 1) * B, j * B : (j + 1) * B] = refs[owner][slot * B : (slot + 1) * B, :] * scale

    for r0 in (0, HALF):
        r1 = r0 + HALF
        p[r0:r1, :] = dot(x_ref[r0:r1, :r1], c[:r1, :])
    out_ref[...] = t_ref[...] - dot(q_ref[...], p[...])


def update(row_count, core, x, cm, co, q, t):
    wide = pltpu.VMEM((NP * B, NC * B), jnp.float32)
    return pl.pallas_call(
        lambda *refs: update_kernel(row_count, *refs),
        out_shape=jax.ShapeDtypeStruct(t.shape, jnp.float32),
        in_specs=[SM] + [VM] * 5, out_specs=VM,
        scratch_shapes=[wide, wide],
        cost_estimate=pl.CostEstimate(flops=3_000_000_000, bytes_accessed=4 << 20, transcendentals=0),
        compiler_params=ROOM, name="update",
    )(core, x, cm, co, q, t)


ALL = ("y", "x", "c", "z")


def device(y, x, c, z):
    return ((y * 4 + x) * 2 + c) * 8 + z


PLANES = [[device(y, x, 0, z) for y in range(8) for x in range(4)] for z in range(8)] + [
    [device(y, x, 1, z) for z in range(8) for x in range(4)] for y in range(8)
]
LINES = [[device(y, x, 0, z) for z in range(8)] for y in range(8) for x in range(4)] + [
    [device(y, x, 1, z) for y in range(8)] for z in range(8) for x in range(4)
]


def reduce_over_devices(keep, send):
    half = keep + lax.ppermute(send, "c", [(0, 1), (1, 0)])
    mine = jnp.sum(lax.all_to_all(half, ALL, 0, 0, axis_index_groups=PLANES), axis=0)
    parts = lax.all_to_all(jnp.broadcast_to(mine[None], (8,) + mine.shape), ALL, 0, 0, axis_index_groups=LINES)
    return jnp.sum(parts, axis=0)


def spread(mine):
    copies = jnp.broadcast_to(mine[None], (PARTS,) + mine.shape)
    half = lax.all_to_all(copies, ALL, 0, 0, axis_index_groups=PLANES)
    half = half.reshape(-1, B)
    return half, lax.ppermute(half, "c", [(0, 1), (1, 0)])


def local(row_count, panel_block, trailing):
    core = lax.axis_index("c").astype(jnp.int32).reshape(1)
    mine = reduce_over_devices(*gram(core, panel_block, trailing))
    mine_g, mine_c = lax.optimization_barrier((mine[:G_ROWS], mine[G_ROWS:]))
    gm, go = spread(mine_g)
    cm, co = spread(mine_c)
    x, r = factor(row_count, core, gm, go)
    return r, update(row_count, core, x, cm, co, basis(x, panel_block), trailing)


def solution(mesh):
    fine = Mesh(mesh.devices.reshape(8, 4, 2, 8), ("y", "x", "c", "z"))
    axes = ("y", "x", "c", "z")

    def run(panel_block, trailing):
        rows = panel_block.shape[0]
        f = jax.shard_map(
            lambda a, t: local(rows, a, t),
            mesh=fine,
            in_specs=(P(axes, None), P(axes, None)),
            out_specs=(P(), P(axes, None)),
            check_vma=False,
        )
        return f(panel_block, trailing)

    return run
```

```python
import jax
import jax.numpy as jnp
from jax import lax
from jax.experimental import pallas as pl
from jax.experimental.pallas import tpu as pltpu
from jax.sharding import Mesh, PartitionSpec as P

HI = lax.Precision.HIGHEST
B = 128
NP = 4
NC = 6
G_BLOCKS = [(i, j) for i in range(NP) for j in range(i, NP)]
C_BLOCKS = [(i, j) for i in range(NP) for j in range(NC)]
G_HALF = 6
C_HALF = 12
VM = pl.BlockSpec(memory_space=pltpu.VMEM)
SM = pl.BlockSpec(memory_space=pltpu.SMEM)


def split_half(blocks):
    n = (len(blocks) + 1) // 2
    return [(b, 0 if k < n else 1, k if k < n else k - n) for k, b in enumerate(blocks)]


PARTS = 32
ROOM = pltpu.CompilerParams(vmem_limit_bytes=20 << 20)
G_ROWS = G_HALF * B // PARTS
C_ROWS = C_HALF * B // PARTS


def products(mine, core, a_ref, t_ref, out_ref):
    g_place = {b: (owner, slot) for b, owner, slot in split_half(G_BLOCKS)}
    c_place = {b: (owner, slot) for b, owner, slot in split_half(C_BLOCKS)}

    def put(value, slot, start, rows):
        for p in range(0, B, 8):
            part, at = divmod(slot * B + p, rows)
            out_ref[part, start + at : start + at + 8, :] = value[p : p + 8]

    def fill(me):
        owner = me if mine else 1 - me
        for i in range(NP):
            cols = [j for j in range(i, NP) if g_place[(i, j)][0] == owner]
            if cols:
                lo, hi = min(cols), max(cols) + 1
                g = dot_t(a_ref[:, i * B : (i + 1) * B], a_ref[:, lo * B : hi * B])
                for j in cols:
                    put(g[:, (j - lo) * B : (j - lo + 1) * B], g_place[(i, j)][1], 0, G_ROWS)
        put(jnp.zeros((B, B), jnp.float32), G_HALF - 1, 0, G_ROWS)
        for i in range(NP):
            cols = [j for j in range(NC) if c_place[(i, j)][0] == owner]
            if cols:
                lo, hi = min(cols), max(cols) + 1
                c = dot_t(a_ref[:, i * B : (i + 1) * B], t_ref[:, lo * B : hi * B])
                for j in cols:
                    put(c[:, (j - lo) * B : (j - lo + 1) * B], c_place[(i, j)][1], G_ROWS, C_ROWS)

    for me in range(2):
        pl.when(core == me)(lambda me=me: fill(me))


def send_kernel(core_ref, a_ref, t_ref, out_ref):
    products(False, core_ref[0], a_ref, t_ref, out_ref)


def keep_kernel(core_ref, a_ref, t_ref, out_ref):
    products(True, core_ref[0], a_ref, t_ref, out_ref)


def gram(core, a, t):
    return [
        pl.pallas_call(
            kernel,
            out_shape=jax.ShapeDtypeStruct((PARTS, G_ROWS + C_ROWS, B), jnp.float32),
            in_specs=[SM, VM, VM], out_specs=VM,
            cost_estimate=pl.CostEstimate(flops=192 * 512 * 1280, bytes_accessed=2 << 20, transcendentals=0),
            compiler_params=ROOM,
        )(core, a, t)
        for kernel in (keep_kernel, send_kernel)
    ]


def stack_pieces(u, order):
    high = u.astype(jnp.bfloat16).astype(jnp.float32)
    rest = u - high
    mid = rest.astype(jnp.bfloat16).astype(jnp.float32)
    part = (high, mid, rest - mid)
    return jnp.concatenate([part[k] for k in order], axis=0).astype(jnp.bfloat16)


LEFT = (0, 0, 1, 0, 2, 1)
RIGHT = (0, 1, 0, 2, 0, 1)


def row_of(v, t):
    return jnp.broadcast_to(v[t : t + 1, :], v.shape)


def lane_of(v, index):
    return jnp.take_along_axis(v, index, axis=1, mode="promise_in_bounds")


def eliminate(w_rows, v_rows, w_next, v_next, base):
    sub = lax.broadcasted_iota(jnp.int32, (8, B), 0)
    ahead = jnp.minimum(base + 8 + sub, B - 1)
    d = {}
    for k in range(8):
        col = lane_of(w_rows, jnp.full((8, B), base + k, jnp.int32))
        for i in range(k + 1):
            d[i, k] = row_of(col, i)
    w = [row_of(w_rows, t) for t in range(8)]
    v = [row_of(v_rows, t) for t in range(8)]
    for t in range(8):
        inv = lax.rsqrt(d[t, t])
        u = {k: d[t, k] * inv for k in range(t + 1, 8)}
        for i in range(t + 1, 8):
            for k in range(i, 8):
                d[i, k] = d[i, k] - u[i] * u[k]
        w[t] = w[t] * inv
        v[t] = v[t] * inv
        for i in range(t + 1, 8):
            w[i] = w[i] - u[i] * w[t]
            v[i] = v[i] - u[i] * v[t]
        weight = lane_of(w[t], ahead)
        w_next = w_next - weight * w[t]
        v_next = v_next - weight * v[t]
    wo, vo = w[0], v[0]
    for t in range(1, 8):
        wo = jnp.where(sub == t, w[t], wo)
        vo = jnp.where(sub == t, v[t], vo)
    return wo, vo, w_next, v_next


def apply_rows(w, v, w_next, v_next, base):
    sub = lax.broadcasted_iota(jnp.int32, (8, B), 0)
    ahead = jnp.minimum(base + 8 + sub, B - 1)
    for t in range(8):
        row = row_of(w, t)
        weight = lane_of(row, ahead)
        w_next = w_next - weight * row
        v_next = v_next - weight * row_of(v, t)
    return w_next, v_next


def diag_factor(s, e, rkk, lkk):
    lane = lax.broadcasted_iota(jnp.int32, (8, B), 1)
    sub = lax.broadcasted_iota(jnp.int32, (8, B), 0)
    zero = jnp.zeros((8, B), jnp.float32)
    e[:B, :] = jnp.where(
        lax.broadcasted_iota(jnp.int32, (B, B), 0) == lax.broadcasted_iota(jnp.int32, (B, B), 1), 1.0, 0.0
    ).astype(jnp.float32)
    s[B:, :] = zero
    e[B:, :] = zero

    def body(g, carry):
        w, v, w_last, v_last = carry
        base = pl.multiple_of(g * 8, 8)
        rows = pl.ds(base, 8)
        after = pl.ds(base + 8, 8)
        left = stack_pieces(w_last, LEFT)
        right = jnp.concatenate([stack_pieces(w_last, RIGHT), stack_pieces(v_last, RIGHT)], axis=1)
        change = lax.dot_general(left, right, (((0,), (0,)), ((), ())), preferred_element_type=jnp.float32)
        w_next, v_next = apply_rows(w_last, v_last, s[after, :], e[after, :], base)
        w, v, w_next, v_next = eliminate(w, v, w_next, v_next, base)
        rkk[rows, :] = jnp.where(lane >= sub + base, w, 0.0)
        lkk[rows, :] = v
        s[:B, :] = s[:B, :] - change[:, :B]
        e[:B, :] = e[:B, :] - change[:, B:]
        return w_next, v_next, w, v

    lax.fori_loop(0, B // 8, body, (s[:8, :], e[:8, :], zero, zero))


def dot(x, y):
    return jnp.dot(x, y, precision=HI, preferred_element_type=jnp.float32)


def dot_t(x, y):
    return lax.dot_general(x, y, (((0,), (0,)), ((), ())), precision=HI, preferred_element_type=jnp.float32)


def panel_step(k, x, rkk, s, e, lkk):
    r0 = k * B
    r1 = r0 + B
    s[:B, :] = x[r0:r1, r0:r1]
    diag_factor(s, e, rkk, lkk)
    linv = lkk[...]
    if k == NP - 1:
        x[r0:, :r0] = dot(linv, x[r0:, :r0])
    else:
        x[r0:r1, :] = dot(linv, x[r0:r1, :])
    x[r0:r1, r0:r1] = linv
    if k < NP - 1:
        change = dot_t(x[r0:r1, r1:], x[r0:r1, :])
        for i in range(k + 1, NP):
            c0 = i * B
            part = change[c0 - r1 : c0 - r1 + B]
            x[c0 : c0 + B, c0:] = x[c0 : c0 + B, c0:] - part[:, c0:]
            if k > 0:
                x[c0 : c0 + B, :r0] = x[c0 : c0 + B, :r0] - part[:, :r0]
            x[c0 : c0 + B, r0:r1] = -part[:, r0:r1]


def factor_kernel(row_count, core_ref, gm_ref, go_ref, x_ref, r_ref, s, e, lkk):
    scale = 1.0 / row_count
    for me in range(2):

        @pl.when(core_ref[0] == me)
        def _(me=me):
            refs = (gm_ref, go_ref) if me == 0 else (go_ref, gm_ref)
            for (i, j), owner, slot in split_half(G_BLOCKS):
                x_ref[i * B : (i + 1) * B, j * B : (j + 1) * B] = refs[owner][slot * B : (slot + 1) * B, :] * scale

    for i in range(NP):
        rows = slice(i * B, (i + 1) * B)
        if i > 0:
            x_ref[rows, : i * B] = jnp.zeros((B, i * B), jnp.float32)
            r_ref[rows, : i * B] = jnp.zeros((B, i * B), jnp.float32)
    for k in range(NP):
        r0, r1 = k * B, (k + 1) * B
        panel_step(k, x_ref, r_ref.at[pl.ds(r0, B), pl.ds(r0, B)], s, e, lkk)
        if r1 < NP * B:
            r_ref[r0:r1, r1:] = x_ref[r0:r1, r1:]
    for i in (0, 2):
        x_ref[i * B : (i + 1) * B, (i + 1) * B : (i + 2) * B] = jnp.zeros((B, B), jnp.float32)


def factor(row_count, core, gm, go):
    full = jax.ShapeDtypeStruct((NP * B, NP * B), jnp.float32)
    return pl.pallas_call(
        lambda *refs: factor_kernel(row_count, *refs),
        out_shape=(full, full), in_specs=[SM, VM, VM], out_specs=[VM, VM],
        scratch_shapes=[pltpu.VMEM((B + 8, B), jnp.float32)] * 2 + [pltpu.VMEM((B, B), jnp.float32)],
        cost_estimate=pl.CostEstimate(flops=8_000_000_000, bytes_accessed=2 << 20, transcendentals=0),
        compiler_params=ROOM, name="factor",
    )(core, gm, go)


HALF = NP * B // 2


def basis_kernel(x_ref, a_ref, q_ref):
    for r0 in (0, HALF):
        r1 = r0 + HALF
        q_ref[:, r0:r1] = lax.dot_general(
            a_ref[:, :r1], x_ref[r0:r1, :r1], (((1,), (1,)), ((), ())), precision=HI, preferred_element_type=jnp.float32
        )


def basis(x, a):
    return pl.pallas_call(
        basis_kernel,
        out_shape=jax.ShapeDtypeStruct(a.shape, jnp.float32), in_specs=[VM, VM], out_specs=VM,
        cost_estimate=pl.CostEstimate(flops=1_000_000_000, bytes_accessed=2 << 20, transcendentals=0),
        compiler_params=ROOM, name="basis",
    )(x, a)


def update_kernel(row_count, core_ref, x_ref, cm_ref, co_ref, q_ref, t_ref, out_ref, c, p):
    scale = 1.0 / row_count
    for me in range(2):

        @pl.when(core_ref[0] == me)
        def _(me=me):
            refs = (cm_ref, co_ref) if me == 0 else (co_ref, cm_ref)
            for (i, j), owner, slot in split_half(C_BLOCKS):
                c[i * B : (i + 1) * B, j * B : (j + 1) * B] = refs[owner][slot * B : (slot + 1) * B, :] * scale

    for r0 in (0, HALF):
        r1 = r0 + HALF
        p[r0:r1, :] = dot(x_ref[r0:r1, :r1], c[:r1, :])
    out_ref[...] = t_ref[...] - dot(q_ref[...], p[...])


def update(row_count, core, x, cm, co, q, t):
    wide = pltpu.VMEM((NP * B, NC * B), jnp.float32)
    return pl.pallas_call(
        lambda *refs: update_kernel(row_count, *refs),
        out_shape=jax.ShapeDtypeStruct(t.shape, jnp.float32),
        in_specs=[SM] + [VM] * 5, out_specs=VM,
        scratch_shapes=[wide, wide],
        cost_estimate=pl.CostEstimate(flops=3_000_000_000, bytes_accessed=4 << 20, transcendentals=0),
        compiler_params=ROOM, name="update",
    )(core, x, cm, co, q, t)


ALL = ("y", "x", "c", "z")


def device(y, x, c, z):
    return ((y * 4 + x) * 2 + c) * 8 + z


PLANES = [[device(y, x, 0, z) for y in range(8) for x in range(4)] for z in range(8)] + [
    [device(y, x, 1, z) for z in range(8) for x in range(4)] for y in range(8)
]
LINES = [[device(y, x, 0, z) for z in range(8)] for y in range(8) for x in range(4)] + [
    [device(y, x, 1, z) for y in range(8)] for z in range(8) for x in range(4)
]


def reduce_over_devices(keep, send):
    half = keep + lax.ppermute(send, "c", [(0, 1), (1, 0)])
    mine = jnp.sum(lax.all_to_all(half, ALL, 0, 0, axis_index_groups=PLANES), axis=0)
    parts = lax.all_to_all(jnp.broadcast_to(mine[None], (8,) + mine.shape), ALL, 0, 0, axis_index_groups=LINES)
    return jnp.sum(parts, axis=0)


def spread(mine):
    copies = jnp.broadcast_to(mine[None], (PARTS,) + mine.shape)
    half = lax.all_to_all(copies, ALL, 0, 0, axis_index_groups=PLANES)
    half = half.reshape(-1, B)
    return half, lax.ppermute(half, "c", [(0, 1), (1, 0)])


def local(row_count, panel_block, trailing):
    core = lax.axis_index("c").astype(jnp.int32).reshape(1)
    mine = reduce_over_devices(*gram(core, panel_block, trailing))
    mine_g, mine_c = lax.optimization_barrier((mine[:G_ROWS], mine[G_ROWS:]))
    gm, go = spread(mine_g)
    cm, co = spread(mine_c)
    x, r = factor(row_count, core, gm, go)
    return r, update(row_count, core, x, cm, co, basis(x, panel_block), trailing)


def solution(mesh):
    fine = Mesh(mesh.devices.reshape(8, 4, 2, 8), ("y", "x", "c", "z"))
    axes = ("y", "x", "c", "z")

    def run(panel_block, trailing):
        rows = panel_block.shape[0]
        f = jax.shard_map(
            lambda a, t: local(rows, a, t),
            mesh=fine,
            in_specs=(P(axes, None), P(axes, None)),
            out_specs=(P(), P(axes, None)),
            check_vma=False,
        )
        return f(panel_block, trailing)

    return run
```

```python
import jax
import jax.numpy as jnp
from jax import lax
from jax.experimental import pallas as pl
from jax.experimental.pallas import tpu as pltpu
from jax.sharding import Mesh, PartitionSpec as P

HI = lax.Precision.HIGHEST
B = 128
NP = 4
NC = 6
G_BLOCKS = [(i, j) for i in range(NP) for j in range(i, NP)]
C_BLOCKS = [(i, j) for j in range(NC) for i in range(NP)]
G_HALF = 6
C_HALF = 12
VM = pl.BlockSpec(memory_space=pltpu.VMEM)
SM = pl.BlockSpec(memory_space=pltpu.SMEM)


def split_half(blocks):
    n = (len(blocks) + 1) // 2
    return [(b, 0 if k < n else 1, k if k < n else k - n) for k, b in enumerate(blocks)]


PARTS = 32
ROOM = pltpu.CompilerParams(vmem_limit_bytes=20 << 20)
G_ROWS = G_HALF * B // PARTS
C_ROWS = C_HALF * B // PARTS


def products(mine, core, a_ref, t_ref, out_ref):
    g_place = {b: (owner, slot) for b, owner, slot in split_half(G_BLOCKS)}
    c_place = {b: (owner, slot) for b, owner, slot in split_half(C_BLOCKS)}

    def put(value, slot, start, rows):
        for p in range(0, B, 8):
            part, at = divmod(slot * B + p, rows)
            out_ref[part, start + at : start + at + 8, :] = value[p : p + 8]

    def fill(me):
        owner = me if mine else 1 - me
        for i in range(NP):
            cols = [j for j in range(i, NP) if g_place[(i, j)][0] == owner]
            if cols:
                lo, hi = min(cols), max(cols) + 1
                g = dot_t(a_ref[:, i * B : (i + 1) * B], a_ref[:, lo * B : hi * B])
                for j in cols:
                    put(g[:, (j - lo) * B : (j - lo + 1) * B], g_place[(i, j)][1], 0, G_ROWS)
        put(jnp.zeros((B, B), jnp.float32), G_HALF - 1, 0, G_ROWS)
        for i in range(NP):
            cols = [j for j in range(NC) if c_place[(i, j)][0] == owner]
            if cols:
                lo, hi = min(cols), max(cols) + 1
                c = dot_t(a_ref[:, i * B : (i + 1) * B], t_ref[:, lo * B : hi * B])
                for j in cols:
                    put(c[:, (j - lo) * B : (j - lo + 1) * B], c_place[(i, j)][1], G_ROWS, C_ROWS)

    for me in range(2):
        pl.when(core == me)(lambda me=me: fill(me))


def send_kernel(core_ref, a_ref, t_ref, out_ref):
    products(False, core_ref[0], a_ref, t_ref, out_ref)


def keep_kernel(core_ref, a_ref, t_ref, out_ref):
    products(True, core_ref[0], a_ref, t_ref, out_ref)


def gram(core, a, t):
    return [
        pl.pallas_call(
            kernel,
            out_shape=jax.ShapeDtypeStruct((PARTS, G_ROWS + C_ROWS, B), jnp.float32),
            in_specs=[SM, VM, VM], out_specs=VM,
            cost_estimate=pl.CostEstimate(flops=192 * 512 * 1280, bytes_accessed=2 << 20, transcendentals=0),
            compiler_params=ROOM,
        )(core, a, t)
        for kernel in (keep_kernel, send_kernel)
    ]


def stack_pieces(u, order):
    high = u.astype(jnp.bfloat16).astype(jnp.float32)
    rest = u - high
    mid = rest.astype(jnp.bfloat16).astype(jnp.float32)
    part = (high, mid, rest - mid)
    return jnp.concatenate([part[k] for k in order], axis=0).astype(jnp.bfloat16)


LEFT = (0, 0, 1, 0, 2, 1)
RIGHT = (0, 1, 0, 2, 0, 1)


def row_of(v, t):
    return jnp.broadcast_to(v[t : t + 1, :], v.shape)


def lane_of(v, index):
    return jnp.take_along_axis(v, index, axis=1, mode="promise_in_bounds")


def eliminate(w_rows, v_rows, w_next, v_next, base):
    sub = lax.broadcasted_iota(jnp.int32, (8, B), 0)
    ahead = jnp.minimum(base + 8 + sub, B - 1)
    d = {}
    for k in range(8):
        col = lane_of(w_rows, jnp.full((8, B), base + k, jnp.int32))
        for i in range(k + 1):
            d[i, k] = row_of(col, i)
    w = [row_of(w_rows, t) for t in range(8)]
    v = [row_of(v_rows, t) for t in range(8)]
    for t in range(8):
        inv = lax.rsqrt(d[t, t])
        u = {k: d[t, k] * inv for k in range(t + 1, 8)}
        for i in range(t + 1, 8):
            for k in range(i, 8):
                d[i, k] = d[i, k] - u[i] * u[k]
        w[t] = w[t] * inv
        v[t] = v[t] * inv
        for i in range(t + 1, 8):
            w[i] = w[i] - u[i] * w[t]
            v[i] = v[i] - u[i] * v[t]
        weight = lane_of(w[t], ahead)
        w_next = w_next - weight * w[t]
        v_next = v_next - weight * v[t]
    wo, vo = w[0], v[0]
    for t in range(1, 8):
        wo = jnp.where(sub == t, w[t], wo)
        vo = jnp.where(sub == t, v[t], vo)
    return wo, vo, w_next, v_next


def apply_rows(w, v, w_next, v_next, base):
    sub = lax.broadcasted_iota(jnp.int32, (8, B), 0)
    ahead = jnp.minimum(base + 8 + sub, B - 1)
    for t in range(8):
        row = row_of(w, t)
        weight = lane_of(row, ahead)
        w_next = w_next - weight * row
        v_next = v_next - weight * row_of(v, t)
    return w_next, v_next


def diag_factor(s, e, rkk, lkk):
    lane = lax.broadcasted_iota(jnp.int32, (8, B), 1)
    sub = lax.broadcasted_iota(jnp.int32, (8, B), 0)
    zero = jnp.zeros((8, B), jnp.float32)
    e[:B, :] = jnp.where(
        lax.broadcasted_iota(jnp.int32, (B, B), 0) == lax.broadcasted_iota(jnp.int32, (B, B), 1), 1.0, 0.0
    ).astype(jnp.float32)
    s[B:, :] = zero
    e[B:, :] = zero

    def body(g, carry):
        w, v, w_last, v_last = carry
        base = pl.multiple_of(g * 8, 8)
        rows = pl.ds(base, 8)
        after = pl.ds(base + 8, 8)
        left = stack_pieces(w_last, LEFT)
        right = jnp.concatenate([stack_pieces(w_last, RIGHT), stack_pieces(v_last, RIGHT)], axis=1)
        change = lax.dot_general(left, right, (((0,), (0,)), ((), ())), preferred_element_type=jnp.float32)
        w_next, v_next = apply_rows(w_last, v_last, s[after, :], e[after, :], base)
        w, v, w_next, v_next = eliminate(w, v, w_next, v_next, base)
        rkk[rows, :] = jnp.where(lane >= sub + base, w, 0.0)
        lkk[rows, :] = v
        s[:B, :] = s[:B, :] - change[:, :B]
        e[:B, :] = e[:B, :] - change[:, B:]
        return w_next, v_next, w, v

    lax.fori_loop(0, B // 8, body, (s[:8, :], e[:8, :], zero, zero))


def dot(x, y):
    return jnp.dot(x, y, precision=HI, preferred_element_type=jnp.float32)


def dot_t(x, y):
    return lax.dot_general(x, y, (((0,), (0,)), ((), ())), precision=HI, preferred_element_type=jnp.float32)


def panel_step(k, x, rkk, s, e, lkk):
    r0 = k * B
    r1 = r0 + B
    s[:B, :] = x[r0:r1, r0:r1]
    diag_factor(s, e, rkk, lkk)
    linv = lkk[...]
    if k == NP - 1:
        x[r0:, :r0] = dot(linv, x[r0:, :r0])
    else:
        x[r0:r1, :] = dot(linv, x[r0:r1, :])
    x[r0:r1, r0:r1] = linv
    if k < NP - 1:
        change = dot_t(x[r0:r1, r1:], x[r0:r1, :])
        for i in range(k + 1, NP):
            c0 = i * B
            part = change[c0 - r1 : c0 - r1 + B]
            x[c0 : c0 + B, c0:] = x[c0 : c0 + B, c0:] - part[:, c0:]
            if k > 0:
                x[c0 : c0 + B, :r0] = x[c0 : c0 + B, :r0] - part[:, :r0]
            x[c0 : c0 + B, r0:r1] = -part[:, r0:r1]


def factor_kernel(row_count, core_ref, gm_ref, go_ref, x_ref, r_ref, s, e, lkk):
    scale = 1.0 / row_count
    for me in range(2):

        @pl.when(core_ref[0] == me)
        def _(me=me):
            refs = (gm_ref, go_ref) if me == 0 else (go_ref, gm_ref)
            for (i, j), owner, slot in split_half(G_BLOCKS):
                x_ref[i * B : (i + 1) * B, j * B : (j + 1) * B] = refs[owner][slot * B : (slot + 1) * B, :] * scale

    for i in range(NP):
        rows = slice(i * B, (i + 1) * B)
        if i > 0:
            x_ref[rows, : i * B] = jnp.zeros((B, i * B), jnp.float32)
            r_ref[rows, : i * B] = jnp.zeros((B, i * B), jnp.float32)
    for k in range(NP):
        r0, r1 = k * B, (k + 1) * B
        panel_step(k, x_ref, r_ref.at[pl.ds(r0, B), pl.ds(r0, B)], s, e, lkk)
        if r1 < NP * B:
            r_ref[r0:r1, r1:] = x_ref[r0:r1, r1:]
    for i in (0, 2):
        x_ref[i * B : (i + 1) * B, (i + 1) * B : (i + 2) * B] = jnp.zeros((B, B), jnp.float32)


def factor(row_count, core, gm, go):
    full = jax.ShapeDtypeStruct((NP * B, NP * B), jnp.float32)
    return pl.pallas_call(
        lambda *refs: factor_kernel(row_count, *refs),
        out_shape=(full, full), in_specs=[SM, VM, VM], out_specs=[VM, VM],
        scratch_shapes=[pltpu.VMEM((B + 8, B), jnp.float32)] * 2 + [pltpu.VMEM((B, B), jnp.float32)],
        cost_estimate=pl.CostEstimate(flops=8_000_000_000, bytes_accessed=2 << 20, transcendentals=0),
        compiler_params=ROOM, name="factor",
    )(core, gm, go)


HALF = NP * B // 2


WIDTH = NC * B // 2


def project_kernel(row_count, x_ref, c_ref, p_ref, c):
    for j in range(NC // 2):
        c[:, j * B : (j + 1) * B] = c_ref[j * NP * B : (j + 1) * NP * B, :] * (1.0 / row_count)
    for r0 in (0, HALF):
        r1 = r0 + HALF
        p_ref[r0:r1, :] = dot(x_ref[r0:r1, :r1], c[:r1, :])


def project(row_count, x, c):
    shape = (NP * B, WIDTH)
    return pl.pallas_call(
        lambda *refs: project_kernel(row_count, *refs),
        out_shape=jax.ShapeDtypeStruct(shape, jnp.float32), in_specs=[VM, VM], out_specs=VM,
        scratch_shapes=[pltpu.VMEM(shape, jnp.float32)],
        cost_estimate=pl.CostEstimate(flops=1_500_000_000, bytes_accessed=2 << 20, transcendentals=0),
        compiler_params=ROOM, name="project",
    )(x, c)


def columns(core):
    return slice(core * WIDTH, (core + 1) * WIDTH)


def basis_kernel(core_ref, x_ref, a_ref, p_ref, t_ref, q_ref, own_ref):
    for r0 in (0, HALF):
        r1 = r0 + HALF
        q_ref[:, r0:r1] = lax.dot_general(
            a_ref[:, :r1], x_ref[r0:r1, :r1], (((1,), (1,)), ((), ())), precision=HI, preferred_element_type=jnp.float32
        )
    own = dot(q_ref[...], p_ref[...])
    for me in range(2):

        @pl.when(core_ref[0] == me)
        def _(me=me):
            own_ref[...] = t_ref[:, columns(me)] - own


def basis(core, x, a, p, t):
    return pl.pallas_call(
        basis_kernel,
        out_shape=(jax.ShapeDtypeStruct(a.shape, jnp.float32), jax.ShapeDtypeStruct((t.shape[0], WIDTH), jnp.float32)),
        in_specs=[SM] + [VM] * 4, out_specs=[VM, VM],
        cost_estimate=pl.CostEstimate(flops=1_500_000_000, bytes_accessed=2 << 20, transcendentals=0),
        compiler_params=ROOM, name="basis",
    )(core, x, a, p, t)


def update_kernel(core_ref, q_ref, p_ref, own_ref, t_ref, out_ref):
    other = dot(q_ref[...], p_ref[...])
    for me in range(2):

        @pl.when(core_ref[0] == me)
        def _(me=me):
            out_ref[:, columns(me)] = own_ref[...]
            out_ref[:, columns(1 - me)] = t_ref[:, columns(1 - me)] - other


def update(core, q, p, own, t):
    return pl.pallas_call(
        update_kernel,
        out_shape=jax.ShapeDtypeStruct(t.shape, jnp.float32),
        in_specs=[SM] + [VM] * 4, out_specs=VM,
        cost_estimate=pl.CostEstimate(flops=500_000_000, bytes_accessed=2 << 20, transcendentals=0),
        compiler_params=ROOM, name="update",
    )(core, q, p, own, t)


ALL = ("y", "x", "c", "z")


def device(y, x, c, z):
    return ((y * 4 + x) * 2 + c) * 8 + z


PLANES = [[device(y, x, 0, z) for y in range(8) for x in range(4)] for z in range(8)] + [
    [device(y, x, 1, z) for z in range(8) for x in range(4)] for y in range(8)
]
LINES = [[device(y, x, 0, z) for z in range(8)] for y in range(8) for x in range(4)] + [
    [device(y, x, 1, z) for y in range(8)] for z in range(8) for x in range(4)
]


def reduce_over_devices(keep, send):
    half = keep + lax.ppermute(send, "c", [(0, 1), (1, 0)])
    mine = jnp.sum(lax.all_to_all(half, ALL, 0, 0, axis_index_groups=PLANES), axis=0)
    parts = lax.all_to_all(jnp.broadcast_to(mine[None], (8,) + mine.shape), ALL, 0, 0, axis_index_groups=LINES)
    return jnp.sum(parts, axis=0)


def spread(mine):
    copies = jnp.broadcast_to(mine[None], (PARTS,) + mine.shape)
    return lax.all_to_all(copies, ALL, 0, 0, axis_index_groups=PLANES).reshape(-1, B)


def from_partner(x):
    return lax.ppermute(x, "c", [(0, 1), (1, 0)])


def local(row_count, panel_block, trailing):
    core = lax.axis_index("c").astype(jnp.int32).reshape(1)
    mine = reduce_over_devices(*gram(core, panel_block, trailing))
    mine_g, mine_c = lax.optimization_barrier((mine[:G_ROWS], mine[G_ROWS:]))
    g = spread(mine_g)
    g_other = from_partner(g)
    c = spread(mine_c)
    x, r = factor(row_count, core, g, g_other)
    p = project(row_count, x, c)
    p_other = from_partner(p)
    q, own = basis(core, x, panel_block, p, trailing)
    return r, update(core, q, p_other, own, trailing)


def solution(mesh):
    fine = Mesh(mesh.devices.reshape(8, 4, 2, 8), ("y", "x", "c", "z"))
    axes = ("y", "x", "c", "z")

    def run(panel_block, trailing):
        rows = panel_block.shape[0]
        f = jax.shard_map(
            lambda a, t: local(rows, a, t),
            mesh=fine,
            in_specs=(P(axes, None), P(axes, None)),
            out_specs=(P(), P(axes, None)),
            check_vma=False,
        )
        return f(panel_block, trailing)

    return run
```

```python
import jax
import jax.numpy as jnp
from jax import lax
from jax.experimental import pallas as pl
from jax.experimental.pallas import tpu as pltpu
from jax.sharding import Mesh, PartitionSpec as P

HI = lax.Precision.HIGHEST
B = 128
NP = 4
NC = 6
G_BLOCKS = [(i, j) for i in range(NP) for j in range(i, NP)]
C_BLOCKS = [(i, j) for j in range(NC) for i in range(NP)]
G_HALF = 6
C_HALF = 12
VM = pl.BlockSpec(memory_space=pltpu.VMEM)
SM = pl.BlockSpec(memory_space=pltpu.SMEM)


def split_half(blocks):
    n = (len(blocks) + 1) // 2
    return [(b, 0 if k < n else 1, k if k < n else k - n) for k, b in enumerate(blocks)]


PARTS = 32
UNROLL = 16
ROOM = pltpu.CompilerParams(vmem_limit_bytes=20 << 20)
G_ROWS = G_HALF * B // PARTS
C_ROWS = C_HALF * B // PARTS


def products(mine, core, a_ref, t_ref, out_ref):
    g_place = {b: (owner, slot) for b, owner, slot in split_half(G_BLOCKS)}
    c_place = {b: (owner, slot) for b, owner, slot in split_half(C_BLOCKS)}

    def put(value, slot, start, rows):
        for p in range(0, B, 8):
            part, at = divmod(slot * B + p, rows)
            out_ref[part, start + at : start + at + 8, :] = value[p : p + 8]

    def fill(me):
        owner = me if mine else 1 - me
        for i in range(NP):
            cols = [j for j in range(i, NP) if g_place[(i, j)][0] == owner]
            if cols:
                lo, hi = min(cols), max(cols) + 1
                g = dot_t(a_ref[:, i * B : (i + 1) * B], a_ref[:, lo * B : hi * B])
                for j in cols:
                    put(g[:, (j - lo) * B : (j - lo + 1) * B], g_place[(i, j)][1], 0, G_ROWS)
        put(jnp.zeros((B, B), jnp.float32), G_HALF - 1, 0, G_ROWS)
        for i in range(NP):
            cols = [j for j in range(NC) if c_place[(i, j)][0] == owner]
            if cols:
                lo, hi = min(cols), max(cols) + 1
                c = dot_t(a_ref[:, i * B : (i + 1) * B], t_ref[:, lo * B : hi * B])
                for j in cols:
                    put(c[:, (j - lo) * B : (j - lo + 1) * B], c_place[(i, j)][1], G_ROWS, C_ROWS)

    for me in range(2):
        pl.when(core == me)(lambda me=me: fill(me))


def send_kernel(core_ref, a_ref, t_ref, out_ref):
    products(False, core_ref[0], a_ref, t_ref, out_ref)


def keep_kernel(core_ref, a_ref, t_ref, out_ref):
    products(True, core_ref[0], a_ref, t_ref, out_ref)


def gram(core, a, t):
    return [
        pl.pallas_call(
            kernel,
            out_shape=jax.ShapeDtypeStruct((PARTS, G_ROWS + C_ROWS, B), jnp.float32),
            in_specs=[SM, VM, VM], out_specs=VM,
            cost_estimate=pl.CostEstimate(flops=192 * 512 * 1280, bytes_accessed=2 << 20, transcendentals=0),
            compiler_params=ROOM,
        )(core, a, t)
        for kernel in (keep_kernel, send_kernel)
    ]


def stack_pieces(u, order):
    high = u.astype(jnp.bfloat16).astype(jnp.float32)
    rest = u - high
    mid = rest.astype(jnp.bfloat16).astype(jnp.float32)
    part = (high, mid, rest - mid)
    return jnp.concatenate([part[k] for k in order], axis=0).astype(jnp.bfloat16)


LEFT = (0, 0, 1, 0, 2, 1)
RIGHT = (0, 1, 0, 2, 0, 1)


def row_of(v, t):
    return jnp.broadcast_to(v[t : t + 1, :], v.shape)


def lane_of(v, index):
    return jnp.take_along_axis(v, index, axis=1, mode="promise_in_bounds")


def next_columns(rows, base):
    return [lane_of(rows, jnp.full((8, B), 0, jnp.int32) + jnp.minimum(base + k, B - 1)) for k in range(8)]


def eliminate(w_rows, v_rows, cols, w_next, v_next, base):
    sub = lax.broadcasted_iota(jnp.int32, (8, B), 0)
    ahead = jnp.minimum(base + 8 + sub, B - 1)
    after = next_columns(w_next, base + 8)
    d = {(i, k): row_of(cols[k], i) for k in range(8) for i in range(k + 1)}
    w = [row_of(w_rows, t) for t in range(8)]
    v = [row_of(v_rows, t) for t in range(8)]
    for t in range(8):
        inv = lax.rsqrt(d[t, t])
        u = {k: d[t, k] * inv for k in range(t + 1, 8)}
        for i in range(t + 1, 8):
            for k in range(i, 8):
                d[i, k] = d[i, k] - u[i] * u[k]
        w[t] = w[t] * inv
        v[t] = v[t] * inv
        for i in range(t + 1, 8):
            w[i] = w[i] - u[i] * w[t]
            v[i] = v[i] - u[i] * v[t]
        weight = lane_of(w[t], ahead)
        w_next = w_next - weight * w[t]
        v_next = v_next - weight * v[t]
        after = [after[k] - weight * row_of(weight, k) for k in range(8)]
    wo, vo = w[0], v[0]
    for t in range(1, 8):
        wo = jnp.where(sub == t, w[t], wo)
        vo = jnp.where(sub == t, v[t], vo)
    return wo, vo, w_next, v_next, after


def apply_rows(w, v, w_next, v_next, base):
    sub = lax.broadcasted_iota(jnp.int32, (8, B), 0)
    ahead = jnp.minimum(base + 8 + sub, B - 1)
    for t in range(8):
        row = row_of(w, t)
        weight = lane_of(row, ahead)
        w_next = w_next - weight * row
        v_next = v_next - weight * row_of(v, t)
    return w_next, v_next


def diag_factor(s, e, rkk, lkk):
    lane = lax.broadcasted_iota(jnp.int32, (8, B), 1)
    sub = lax.broadcasted_iota(jnp.int32, (8, B), 0)
    zero = jnp.zeros((8, B), jnp.float32)
    e[:B, :] = jnp.where(
        lax.broadcasted_iota(jnp.int32, (B, B), 0) == lax.broadcasted_iota(jnp.int32, (B, B), 1), 1.0, 0.0
    ).astype(jnp.float32)
    s[B:, :] = zero
    e[B:, :] = zero

    def body(g, carry):
        w, v, w_last, v_last, cols = carry
        base = pl.multiple_of(g * 8, 8)
        rows = pl.ds(base, 8)
        after = pl.ds(base + 8, 8)
        left = stack_pieces(w_last, LEFT)
        right = jnp.concatenate([stack_pieces(w_last, RIGHT), stack_pieces(v_last, RIGHT)], axis=1)
        change = lax.dot_general(left, right, (((0,), (0,)), ((), ())), preferred_element_type=jnp.float32)
        w_next, v_next = apply_rows(w_last, v_last, s[after, :], e[after, :], base)
        w, v, w_next, v_next, cols = eliminate(w, v, cols, w_next, v_next, base)
        rkk[rows, :] = jnp.where(lane >= sub + base, w, 0.0)
        lkk[rows, :] = v
        s[:B, :] = s[:B, :] - change[:, :B]
        e[:B, :] = e[:B, :] - change[:, B:]
        return w_next, v_next, w, v, cols

    lax.fori_loop(0, B // 8, body, (s[:8, :], e[:8, :], zero, zero, next_columns(s[:8, :], 0)), unroll=UNROLL)


def dot(x, y):
    return jnp.dot(x, y, precision=HI, preferred_element_type=jnp.float32)


def dot_t(x, y):
    return lax.dot_general(x, y, (((0,), (0,)), ((), ())), precision=HI, preferred_element_type=jnp.float32)


def panel_step(k, x, rkk, s, e, lkk):
    r0 = k * B
    r1 = r0 + B
    s[:B, :] = x[r0:r1, r0:r1]
    diag_factor(s, e, rkk, lkk)
    linv = lkk[...]
    if k == NP - 1:
        x[r0:, :r0] = dot(linv, x[r0:, :r0])
    else:
        x[r0:r1, :] = dot(linv, x[r0:r1, :])
    x[r0:r1, r0:r1] = linv
    if k < NP - 1:
        change = dot_t(x[r0:r1, r1:], x[r0:r1, :])
        for i in range(k + 1, NP):
            c0 = i * B
            part = change[c0 - r1 : c0 - r1 + B]
            x[c0 : c0 + B, c0:] = x[c0 : c0 + B, c0:] - part[:, c0:]
            if k > 0:
                x[c0 : c0 + B, :r0] = x[c0 : c0 + B, :r0] - part[:, :r0]
            x[c0 : c0 + B, r0:r1] = -part[:, r0:r1]


def factor_kernel(row_count, core_ref, gm_ref, go_ref, x_ref, r_ref, s, e, lkk):
    scale = 1.0 / row_count
    for me in range(2):

        @pl.when(core_ref[0] == me)
        def _(me=me):
            refs = (gm_ref, go_ref) if me == 0 else (go_ref, gm_ref)
            for (i, j), owner, slot in split_half(G_BLOCKS):
                x_ref[i * B : (i + 1) * B, j * B : (j + 1) * B] = refs[owner][slot * B : (slot + 1) * B, :] * scale

    for i in range(NP):
        rows = slice(i * B, (i + 1) * B)
        if i > 0:
            x_ref[rows, : i * B] = jnp.zeros((B, i * B), jnp.float32)
            r_ref[rows, : i * B] = jnp.zeros((B, i * B), jnp.float32)
    for k in range(NP):
        r0, r1 = k * B, (k + 1) * B
        panel_step(k, x_ref, r_ref.at[pl.ds(r0, B), pl.ds(r0, B)], s, e, lkk)
        if r1 < NP * B:
            r_ref[r0:r1, r1:] = x_ref[r0:r1, r1:]
    for i in (0, 2):
        x_ref[i * B : (i + 1) * B, (i + 1) * B : (i + 2) * B] = jnp.zeros((B, B), jnp.float32)


def factor(row_count, core, gm, go):
    full = jax.ShapeDtypeStruct((NP * B, NP * B), jnp.float32)
    return pl.pallas_call(
        lambda *refs: factor_kernel(row_count, *refs),
        out_shape=(full, full), in_specs=[SM, VM, VM], out_specs=[VM, VM],
        scratch_shapes=[pltpu.VMEM((B + 8, B), jnp.float32)] * 2 + [pltpu.VMEM((B, B), jnp.float32)],
        cost_estimate=pl.CostEstimate(flops=8_000_000_000, bytes_accessed=2 << 20, transcendentals=0),
        compiler_params=ROOM, name="factor",
    )(core, gm, go)


HALF = NP * B // 2


WIDTH = NC * B // 2


def project_kernel(row_count, x_ref, c_ref, p_ref, c):
    for j in range(NC // 2):
        c[:, j * B : (j + 1) * B] = c_ref[j * NP * B : (j + 1) * NP * B, :] * (1.0 / row_count)
    for r0 in (0, HALF):
        r1 = r0 + HALF
        p_ref[r0:r1, :] = dot(x_ref[r0:r1, :r1], c[:r1, :])


def project(row_count, x, c):
    shape = (NP * B, WIDTH)
    return pl.pallas_call(
        lambda *refs: project_kernel(row_count, *refs),
        out_shape=jax.ShapeDtypeStruct(shape, jnp.float32), in_specs=[VM, VM], out_specs=VM,
        scratch_shapes=[pltpu.VMEM(shape, jnp.float32)],
        cost_estimate=pl.CostEstimate(flops=1_500_000_000, bytes_accessed=2 << 20, transcendentals=0),
        compiler_params=ROOM, name="project",
    )(x, c)


def columns(core):
    return slice(core * WIDTH, (core + 1) * WIDTH)


def basis_kernel(core_ref, x_ref, a_ref, p_ref, t_ref, q_ref, own_ref):
    for r0 in (0, HALF):
        r1 = r0 + HALF
        q_ref[:, r0:r1] = lax.dot_general(
            a_ref[:, :r1], x_ref[r0:r1, :r1], (((1,), (1,)), ((), ())), precision=HI, preferred_element_type=jnp.float32
        )
    own = dot(q_ref[...], p_ref[...])
    for me in range(2):

        @pl.when(core_ref[0] == me)
        def _(me=me):
            own_ref[...] = t_ref[:, columns(me)] - own


def basis(core, x, a, p, t):
    return pl.pallas_call(
        basis_kernel,
        out_shape=(jax.ShapeDtypeStruct(a.shape, jnp.float32), jax.ShapeDtypeStruct((t.shape[0], WIDTH), jnp.float32)),
        in_specs=[SM] + [VM] * 4, out_specs=[VM, VM],
        cost_estimate=pl.CostEstimate(flops=1_500_000_000, bytes_accessed=2 << 20, transcendentals=0),
        compiler_params=ROOM, name="basis",
    )(core, x, a, p, t)


def update_kernel(core_ref, q_ref, p_ref, own_ref, t_ref, out_ref):
    other = dot(q_ref[...], p_ref[...])
    for me in range(2):

        @pl.when(core_ref[0] == me)
        def _(me=me):
            out_ref[:, columns(me)] = own_ref[...]
            out_ref[:, columns(1 - me)] = t_ref[:, columns(1 - me)] - other


def update(core, q, p, own, t):
    return pl.pallas_call(
        update_kernel,
        out_shape=jax.ShapeDtypeStruct(t.shape, jnp.float32),
        in_specs=[SM] + [VM] * 4, out_specs=VM,
        cost_estimate=pl.CostEstimate(flops=500_000_000, bytes_accessed=2 << 20, transcendentals=0),
        compiler_params=ROOM, name="update",
    )(core, q, p, own, t)


ALL = ("y", "x", "c", "z")


def device(y, x, c, z):
    return ((y * 4 + x) * 2 + c) * 8 + z


PLANES = [[device(y, x, 0, z) for y in range(8) for x in range(4)] for z in range(8)] + [
    [device(y, x, 1, z) for z in range(8) for x in range(4)] for y in range(8)
]
LINES = [[device(y, x, 0, z) for z in range(8)] for y in range(8) for x in range(4)] + [
    [device(y, x, 1, z) for y in range(8)] for z in range(8) for x in range(4)
]


def reduce_over_devices(keep, send):
    half = keep + lax.ppermute(send, "c", [(0, 1), (1, 0)])
    mine = jnp.sum(lax.all_to_all(half, ALL, 0, 0, axis_index_groups=PLANES), axis=0)
    parts = lax.all_to_all(jnp.broadcast_to(mine[None], (8,) + mine.shape), ALL, 0, 0, axis_index_groups=LINES)
    return jnp.sum(parts, axis=0)


def spread(mine):
    copies = jnp.broadcast_to(mine[None], (PARTS,) + mine.shape)
    return lax.all_to_all(copies, ALL, 0, 0, axis_index_groups=PLANES).reshape(-1, B)


def from_partner(x):
    return lax.ppermute(x, "c", [(0, 1), (1, 0)])


def local(row_count, panel_block, trailing):
    core = lax.axis_index("c").astype(jnp.int32).reshape(1)
    mine = reduce_over_devices(*gram(core, panel_block, trailing))
    mine_g, mine_c = lax.optimization_barrier((mine[:G_ROWS], mine[G_ROWS:]))
    g = spread(mine_g)
    g_other = from_partner(g)
    c = spread(mine_c)
    x, r = factor(row_count, core, g, g_other)
    p = project(row_count, x, c)
    p_other = from_partner(p)
    q, own = basis(core, x, panel_block, p, trailing)
    return r, update(core, q, p_other, own, trailing)


def solution(mesh):
    fine = Mesh(mesh.devices.reshape(8, 4, 2, 8), ("y", "x", "c", "z"))
    axes = ("y", "x", "c", "z")

    def run(panel_block, trailing):
        rows = panel_block.shape[0]
        f = jax.shard_map(
            lambda a, t: local(rows, a, t),
            mesh=fine,
            in_specs=(P(axes, None), P(axes, None)),
            out_specs=(P(), P(axes, None)),
            check_vma=False,
        )
        return f(panel_block, trailing)

    return run
```
